32 devices in a mesh: pairs: 32 (over z, y, x, core).
Axes of the slice: x: 2, y: 2, z: 4, core: 2. Of those that a mesh axis runs over, the one named last changes fastest.
Arguments:
- pno_basis: bfloat16 [256, 192, 128], P('pairs'), may hold values from -0.4375 to 0.4375
- pno_count: int32 [256], P('pairs'), may hold values from 64 to 128
- partner_owner: int32 [256, 12], P('pairs'), may hold values from 0 to 31, all different within a row; in each aligned block of 8 rows (0 to 7, 8 to 15, ...) at most 3 rows name the same one
- partner_local: int32 [256, 12], P('pairs'), may hold values from 0 to 7
- exchange_k: bfloat16 [256, 128, 128], P('pairs'), may hold values from -6 to 6
- ladder_factor: bfloat16 [256, 40, 128, 128], P('pairs'), may hold values from -0.15625 to 0.15625
- pno_energy: float32 [256, 128], P('pairs'), may hold values from 0.3 to 3
- occ_energy: float32 [256], P('pairs'), may hold values from -2 to -0.6
- coupling_fock: bfloat16 [256, 12], P('pairs'), may hold values from -3 to 3
Outputs:
- amplitudes: float32 [256, 128, 128], P('pairs')
The draws below stay inside these ranges and needn't reach their ends.
Inputs may be any that keep to these rules, and one draw needn't show every extreme that they name: `partner_owner`: the 12 partners of one pair have different owners. Among the 8 pairs of one device no device is named more than 3 times, and in some devices' pairs one device is named exactly 3 times. Partner c of pair p is the pair numbered partner_owner[p, c] * 8 + partner_local[p, c]. Pair p uses its first pno_count[p] orbitals; the others are padding.
All inputs are finite; a program needn't handle non-finite values.
Results may differ from the reference program's by a relative error of at most 0.009.
Values may be sent and summed in bfloat16 or wider, within the bound.
A program may use at most 128 MiB of HBM per device.

```python
import math
import jax
import jax.numpy as jnp
import numpy as np
from jax import lax

NPNO = 128
NV = 192
NAUX = 40
NCOUP = 12
ITERS = 3
PAIRS_DEV = 8
PAIRS = 256
MOST = 3
N_PAIRS = 32


def set_ends(result, stream_key, smallest, top_value):
    extent = result.shape
    spot = [jax.random.randint(jax.random.fold_in(stream_key, axis), (), 0, extent[axis]) for axis in range(len(extent))]
    result = result.at[tuple(spot)].set(smallest)
    longest = extent.index(max(extent))
    spot[longest] = (spot[longest] + 1) % extent[longest]
    return result.at[tuple(spot)].set(top_value)


def block_levels(key, dims, shards, least, high):
    level = 1.0
    for dim, parts in shards:
        draws = jax.random.uniform(jax.random.fold_in(jax.random.fold_in(key, 6), dim), (parts,), jnp.float32, least / len(shards), high / len(shards))
        level = level * jnp.repeat(jnp.exp(draws), dims[dim] // parts).reshape((-1,) + (1,) * (len(dims) - 1 - dim))
    return level


def shared_out(rng, own, number, rows, amount, top, bound, skew):
    sequence = jax.random.permutation(rng, amount)
    packed, common = load_shares(amount, rows * top, bound, skew, True), load_shares(amount, rows * top, bound, skew, False)
    places = jnp.arange(amount)

    def named(sizes, turn):
        used = int((sizes > 0).sum())
        fixed = max(1, used // 4)
        passed = fixed + (places - fixed + turn * (used - fixed)) % max(1, amount - fixed)
        return jnp.zeros((amount,), jnp.int32).at[sequence[jnp.where(places < fixed, places, passed)]].set(jnp.asarray(sizes, jnp.int32))

    sizes = jnp.where(number % 4 == 0, named(packed, number // 4), named(common, number - number // 4 - 1))
    mixed = jax.random.permutation(jax.random.fold_in(own, 3), amount)
    giver, taker = mixed[0:amount // 2 * 2:2], mixed[1:amount // 2 * 2:2]
    room = jnp.minimum(sizes[giver] - 1, bound - sizes[taker]) // 2
    room = jnp.where((giver == sequence[0]) | (taker == sequence[0]) | (sizes[taker] == 0), 0, jnp.maximum(room, 0))
    passed = jax.random.randint(jax.random.fold_in(own, 4), (amount // 2,), 0, 1 << 20) % (room + 1)
    sizes = sizes.at[giver].add(-passed).at[taker].add(passed)
    labels = jnp.searchsorted(jnp.cumsum(sizes), jnp.arange(rows * top), side="right").astype(jnp.int32)
    table = labels.reshape(top, rows).T
    table = table[jax.random.permutation(jax.random.fold_in(own, 1), rows)]
    turn = jax.random.randint(jax.random.fold_in(own, 2), (rows, 1), 0, top)
    return jnp.take_along_axis(table, (jnp.arange(top)[None, :] + turn) % top, axis=1)


def load_shares(count, total, bound, lean, full):
    loads = [(1 << 20) // math.isqrt(grade ** lean) + 1 for grade in range(1, count + 1)]
    largest = bound if full else min(bound, max(-(-total // count), total * loads[0] // sum(loads)))
    least = 1 if total - largest >= count - 1 else 0
    given, rest = [largest] + [least] * (count - 1), total - largest - least * (count - 1)
    while rest > 0:
        candidates = [i for i in range(1, count) if given[i] < largest] or [i for i in range(1, count) if given[i] < bound]
        pool, remaining = sum([loads[i] for i in candidates]), rest
        for i in candidates:
            more = min(bound - given[i], max(1, remaining * loads[i] // pool), rest)
            given[i] = given[i] + more
            rest = rest - more
    return np.array(given)


def centred(own_key, extent, spread, limit, split=(), kind=jnp.bfloat16):
    result = jax.random.normal(own_key, extent, jnp.float32) * spread
    if len(split) > 0:
        result = block_levels(own_key, extent, split, -0.22, 0.18) * result
    return jnp.clip(result, min=-limit, max=limit).astype(kind)


def setup_inputs(seed: int = 0) -> dict:
    arg_keys = jax.random.split(jax.random.key(seed), 10)
    pno_basis = centred(arg_keys[0], (PAIRS, NV, NPNO), NV ** -0.5, 0.4375, ((0, 32),))
    pno_count = set_ends(jax.random.randint(arg_keys[1], (PAIRS,), NPNO // 2, NPNO + 1), jax.random.fold_in(arg_keys[1], 1), NPNO // 2, NPNO).astype(jnp.int32)
    partner_owner_keys = jax.random.split(jax.random.fold_in(arg_keys[2], 1), PAIRS // PAIRS_DEV)
    partner_owner_turns = jax.random.permutation(jax.random.fold_in(arg_keys[2], 3), PAIRS // PAIRS_DEV)
    partner_owner = jax.vmap(lambda own, number: shared_out(jax.random.fold_in(arg_keys[2], 2), own, number, PAIRS_DEV, N_PAIRS, NCOUP, MOST, 2))(partner_owner_keys, partner_owner_turns).reshape((PAIRS, NCOUP))
    partner_local = set_ends(jax.random.randint(arg_keys[3], (PAIRS, NCOUP), 0, PAIRS_DEV), jax.random.fold_in(arg_keys[3], 1), 0, PAIRS_DEV - 1).astype(jnp.int32)
    exchange_k = centred(arg_keys[4], (PAIRS, NPNO, NPNO), 1.0, 6.0, ((0, 32),))
    ladder_factor = centred(arg_keys[5], (PAIRS, NAUX, NPNO, NPNO), (NPNO * NAUX // 4) ** -0.5, 0.15625, ((0, 32),))
    pno_energy = jnp.clip(jnp.exp(math.log(3.0) - 2.3025851 * jax.random.uniform(arg_keys[6], (PAIRS, NPNO), jnp.float32) ** block_levels(arg_keys[6], (PAIRS, NPNO), ((0, 32),), -0.2, 0.2)), 0.3, 3.0)
    occ_energy = jnp.clip(-2.0 + 1.4 * jax.random.uniform(arg_keys[7], (PAIRS,), jnp.float32) ** block_levels(arg_keys[7], (PAIRS,), ((0, 32),), -0.2, 0.2), -2.0, -0.6)
    coupling_fock = centred(arg_keys[8], (PAIRS, NCOUP), 0.5, 3.0, ((0, 32),))
    return {"pno_basis": pno_basis, "pno_count": pno_count, "partner_owner": partner_owner, "partner_local": partner_local, "exchange_k": exchange_k, "ladder_factor": ladder_factor, "pno_energy": pno_energy, "occ_energy": occ_energy, "coupling_fock": coupling_fock}


level_shift = 0.3


def reference(pno_basis, pno_count, partner_owner, partner_local, exchange_k, ladder_factor, pno_energy, occ_energy, coupling_fock):
    columns = lax.broadcasted_iota(jnp.int32, (PAIRS, NPNO), 1)
    live_cols = (columns < pno_count[:, None]).astype(jnp.float32)
    masked_basis = (pno_basis.astype(jnp.float32) * live_cols[:, None, :]).astype(jnp.bfloat16)
    partner_ids = (partner_owner * PAIRS_DEV + partner_local).astype(jnp.int32)
    block_count = PAIRS // PAIRS_DEV
    block_numbers = jnp.arange(block_count, dtype=jnp.int32)

    def margin_block(block_index):
        first_row = (block_index * PAIRS_DEV).astype(jnp.int32)
        own_basis = lax.dynamic_slice_in_dim(masked_basis, first_row, PAIRS_DEV, 0).astype(jnp.float32)
        chosen = lax.dynamic_slice_in_dim(partner_ids, first_row, PAIRS_DEV, 0)
        other_basis = masked_basis[chosen].astype(jnp.float32)
        product = jnp.einsum("rva,rcvb->rcab", own_basis, other_basis, precision=lax.Precision.HIGHEST)
        return product.astype(jnp.bfloat16)

    margin = lax.map(margin_block, block_numbers).reshape(PAIRS, NCOUP, NPNO, NPNO)
    energy_sum = pno_energy[:, :, None] + pno_energy[:, None, :] - occ_energy[:, None, None]
    divisor = energy_sum + level_shift
    driving = exchange_k.astype(jnp.float32) * (live_cols[:, :, None] * live_cols[:, None, :])
    amplitudes = -driving / divisor
    weights = coupling_fock.astype(jnp.float32)
    for iteration in range(ITERS):
        sent_amps = amplitudes.astype(jnp.bfloat16)

        def couple_block(block_index):
            first_row = (block_index * PAIRS_DEV).astype(jnp.int32)
            block_margin = lax.dynamic_slice_in_dim(margin, first_row, PAIRS_DEV, 0).astype(jnp.float32)
            chosen = lax.dynamic_slice_in_dim(partner_ids, first_row, PAIRS_DEV, 0)
            block_weights = lax.dynamic_slice_in_dim(weights, first_row, PAIRS_DEV, 0)
            partner_amps = sent_amps[chosen].astype(jnp.float32)
            left_half = jnp.einsum("rcab,rcbd->rcad", block_margin, partner_amps, precision=lax.Precision.HIGHEST)
            left_half = left_half * block_weights[:, :, None, None]
            left_half = lax.optimization_barrier(left_half.astype(jnp.bfloat16)).astype(jnp.float32)
            coupling_terms = jnp.einsum("rcad,rced->rcae", left_half, block_margin, precision=lax.Precision.HIGHEST)
            coupling_terms = lax.optimization_barrier(coupling_terms.astype(jnp.bfloat16)).astype(jnp.float32)
            own_amps = lax.dynamic_slice_in_dim(sent_amps, first_row, PAIRS_DEV, 0).astype(jnp.float32)
            factors = lax.dynamic_slice_in_dim(ladder_factor, first_row, PAIRS_DEV, 0).astype(jnp.float32)
            ladder_half = jnp.einsum("rqac,rcd->rqad", factors, own_amps, precision=lax.Precision.HIGHEST)
            ladder_half = lax.optimization_barrier(ladder_half.astype(jnp.bfloat16)).astype(jnp.float32)
            ladder = jnp.einsum("rqad,rqbd->rab", ladder_half, factors, precision=lax.Precision.HIGHEST)
            return jnp.sum(coupling_terms, axis=1) + ladder

        coupled = lax.map(couple_block, block_numbers).reshape(PAIRS, NPNO, NPNO)
        residual = driving + energy_sum * amplitudes + coupled
        amplitudes = amplitudes - residual / divisor
    return amplitudes
```

```python
import functools
import jax
import jax.numpy as jnp
from jax import lax
from jax.experimental import pallas as pl
from jax.experimental.pallas import tpu as pltpu
from jax.sharding import PartitionSpec as P

ITERS = 3


level_shift = 0.3
VMEM_BYTES = 67043328
MESH = pl.DeviceIdType.MESH


def contract(a, b, da, db):
    return lax.dot_general(a, b, (((da,), (db,)), ((), ())), preferred_element_type=jnp.float32)


GROUP = 8
QUAD = 4
KINDS = ("x", "z", "diag")


def table_rows(slots, own_pairs, ref_owner, ref_local, ref_fock, here):
    owner = ref_owner[...]
    local = ref_local[...]
    fock = ref_fock[...].astype(jnp.float32)
    partners = owner.shape[1]
    lane = lax.broadcasted_iota(jnp.int32, owner.shape, 1)
    row = lax.broadcasted_iota(jnp.int32, owner.shape, 0)
    high = lax.shift_right_logical(owner, 4)
    mid = lax.shift_right_logical(owner, 2) & 1
    place = ((lax.shift_right_logical(owner, 3) & 1) * 4 + (owner & 3)) * own_pairs + local
    slot = lax.broadcasted_iota(jnp.int32, (slots, partners), 0)
    slot_wide = lax.broadcasted_iota(jnp.int32, (slots, 128), 0)
    lane_wide = lax.broadcasted_iota(jnp.int32, (slots, 128), 1)
    my_high, my_mid = here
    found = []
    for b in range(QUAD):
        want_high = my_high if b < 2 else 1 - my_high
        want_mid = my_mid if b % 2 == 0 else 1 - my_mid
        chosen = (high == want_high) & (mid == want_mid)
        ones = jnp.where(chosen, 1, 0)
        before = jnp.zeros_like(ones)
        number = jnp.zeros((own_pairs, 1), jnp.int32)
        for c in range(partners):
            before = before + jnp.where(lane > c, ones[:, c : c + 1], 0)
            number = number + ones[:, c : c + 1]
        ahead = jnp.zeros((own_pairs, partners), jnp.int32)
        wide = jnp.broadcast_to(number, (own_pairs, partners))
        for p in range(own_pairs):
            ahead = ahead + jnp.where(row > p, wide[p : p + 1, :], 0)
        rank = jnp.where(chosen, before + ahead, -1)
        pair = jnp.zeros((slots, partners), jnp.int32)
        other = jnp.zeros((slots, partners), jnp.int32)
        weight = jnp.zeros((slots, partners), jnp.float32)
        begins = jnp.zeros((slots, partners), jnp.float32)
        for p in range(own_pairs):
            hit = rank[p : p + 1, :] == slot
            pair = pair + jnp.where(hit, p, 0)
            other = other + jnp.where(hit, place[p : p + 1, :], 0)
            weight = weight + jnp.where(hit, fock[p : p + 1, :], 0.0)
            begins = jnp.where(ahead[p : p + 1, :] == slot, 1.0, begins)
        sums = [jnp.zeros((slots, 1), v.dtype) for v in (pair, other, weight)]
        for c in range(partners):
            sums = [t + v[:, c : c + 1] for t, v in zip(sums, (pair, other, weight))]
        ints = jnp.where(lane_wide == 0, jnp.broadcast_to(sums[0], (slots, 128)), jnp.broadcast_to(sums[1], (slots, 128)))
        last = jnp.where(number > 0, jnp.minimum(ahead[:, 0:1] + number - 1, slots), slots)
        found.append((
            ints,
            jnp.broadcast_to(last, (own_pairs, 128)),
            jnp.broadcast_to(sums[2], (slots, 128)),
            jnp.broadcast_to(1.0 - begins[:, 0:1], (slots, 128)),
        ))
    return found


def kernel(
    slots, basis_ref, count_ref, owner_ref, local_ref, exchange_ref, ladder_hbm, energy_ref,
    occ_ref, fock_ref, out_ref,
    group_basis, row_own, row_y, row_z, row_yz, amps_a, amps_b, amps_c, factors, margin, sums, ladder,
    from_y, from_z, to_y, to_z, ints_out, ints_in, floats_out, floats_in, table,
    load_sem, recv_sem, recv_sib, send_sem, basis_recv, basis_send, table_recv, table_send, table_load,
    y_recv, z_recv, y_send, z_send,
):
    own_pairs, domain, orbitals = basis_ref.shape
    fitted = factors.shape[1]
    me = lax.axis_index("pairs")
    core = me % 2
    bit_x = me // 2 % 2
    bit_y = me // 4 % 2
    bit_l = me // 8 % 2
    bit_h = me // 16
    sibling = me + 1 - 2 * core
    dev_x = me + 2 * (1 - 2 * bit_x)
    dev_y = me + 4 * (1 - 2 * bit_y)
    dev_l = me + 8 * (1 - 2 * bit_l)
    dev_h = me + 16 * (1 - 2 * bit_h)
    dev_yh = dev_h + 4 * (1 - 2 * bit_y)
    mine = bit_l * 4 + bit_x * 2 + core
    mine_x = bit_l * 4 + (1 - bit_x) * 2 + core
    mine_l = (1 - bit_l) * 4 + bit_x * 2 + core
    mine_d = (1 - bit_l) * 4 + (1 - bit_x) * 2 + core
    rows_basis = (row_own, row_y, row_z, row_yz)
    bufs = (group_basis, amps_a, amps_b, amps_c)
    amps = (amps_a, amps_b, amps_c)
    pieces = own_pairs // 2
    x_first = ((pieces - 1,), (pieces - 1,), (), ())

    loads = [
        pltpu.make_async_copy(ladder_hbm.at[p], factors.at[p], load_sem.at[p])
        for p in range(own_pairs)
    ]

    def span(k):
        return pl.ds(2 * k, 2)

    def push(u, k, owner, dev, sem):
        view = bufs[u].at[owner, span(k)]
        return pltpu.make_async_remote_copy(
            src_ref=view, dst_ref=view, send_sem=send_sem.at[u], recv_sem=sem,
            device_id=(dev,), device_id_type=MESH,
        )

    def own(u, k):
        push(u, k, mine, dev_x, recv_sem.at[u, 0, k]).start()
        push(u, k, mine, dev_l, recv_sem.at[u, 1, k]).start()
        push(u, k, mine, sibling, recv_sib.at[u]).start()

    def came(u, kind, k):
        def go():
            owner = (mine_x, mine_l, mine_d)[kind]
            push(u, k, owner, sibling, recv_sem.at[u, kind, k]).wait_recv()
            if kind == 0 and k in x_first[u]:
                push(u, k, owner, dev_l, recv_sem.at[u, 2, k]).start()
            if kind == 1 and k not in x_first[u]:
                push(u, k, owner, dev_x, recv_sem.at[u, 2, k]).start()
            push(u, k, owner, sibling, recv_sib.at[u]).start()
        return go

    def sibling_done(u):
        view = bufs[u].at[pl.ds(0, GROUP // 2)]
        pltpu.make_async_copy(view, view, recv_sib.at[u]).wait()

    def sends_done(u):
        view = bufs[u].at[pl.ds(0, GROUP - 1)]
        pltpu.make_async_copy(view, view, send_sem.at[u]).wait()

    def push_row(src, b, k, dev):
        return pltpu.make_async_remote_copy(
            src_ref=src.at[span(k)], dst_ref=rows_basis[b].at[span(k)],
            send_sem=basis_send, recv_sem=basis_recv.at[b, k],
            device_id=(dev,), device_id_type=MESH,
        )

    def row_came(b, k):
        def go():
            push_row(row_own, b, k, dev_y).wait_recv()
            if b == 2:
                push_row(row_z, 3, k, dev_y).start()
        return go

    lanes = lax.broadcasted_iota(jnp.int32, (orbitals, orbitals), 1)
    rows = lax.broadcasted_iota(jnp.int32, (orbitals, orbitals), 0)
    energy_cols = jnp.transpose(energy_ref[...])

    def pair_terms(p):
        esum = energy_cols[:, p : p + 1] + energy_ref[p : p + 1, :] - occ_ref[p]
        count = count_ref[p]
        live = (lanes < count) & (rows < count)
        driving = jnp.where(live, exchange_ref[p].astype(jnp.float32), 0.0)
        return esum, esum + level_shift, driving

    barrier = pltpu.get_barrier_semaphore()
    near = (sibling, dev_x, dev_l, dev_y, dev_h, dev_yh)
    for dev in near:
        pl.semaphore_signal(barrier, inc=1, device_id=(dev,), device_id_type=MESH)
    for load in loads:
        load.start()

    basis_lanes = lax.broadcasted_iota(jnp.int32, (domain, orbitals), 1)

    def mask_basis(p):
        held = jnp.where(
            basis_lanes < count_ref[p], basis_ref[p].astype(jnp.float32), 0.0
        ).astype(jnp.bfloat16)
        group_basis[mine, p] = held
        row_own[p] = held

    def first_amps(p):
        esum, divisor, driving = pair_terms(p)
        first = -driving / divisor
        out_ref[p] = first
        amps_a[mine, p] = first.astype(jnp.bfloat16)

    for p in range(own_pairs):
        mask_basis(p)
    pl.semaphore_wait(barrier, len(near))

    for k in range(pieces):
        own(0, k)
        push_row(row_own, 2, k, dev_h).start()
        push_row(row_own, 1, k, dev_y).start()

    for p in range(own_pairs):
        first_amps(p)
    for k in range(pieces):
        own(1, k)

    found = table_rows(slots, own_pairs, owner_ref, local_ref, fock_ref, (bit_h, bit_y))
    for b in range(QUAD):
        ints, last, weight, keep = found[b]
        to_int, to_float = (ints_in, floats_in) if b == 0 else (ints_out, floats_out)
        to_int[b, 0:slots] = ints
        to_int[b, slots : slots + own_pairs] = last
        to_float[b, 0:slots] = weight
        to_float[b, slots : 2 * slots] = keep

    def push_table(b, which):
        src, dst = ((ints_out, ints_in), (floats_out, floats_in))[which]
        return pltpu.make_async_remote_copy(
            src_ref=src.at[b], dst_ref=dst.at[b], send_sem=table_send.at[which, b], recv_sem=table_recv.at[which, b],
            device_id=((dev_y, dev_y, dev_h, dev_yh)[b],), device_id_type=MESH,
        )

    def load_table(b):
        return pltpu.make_async_copy(ints_in.at[b], table.at[b], table_load.at[b])

    for b in range(1, QUAD):
        push_table(b, 0).start()
        push_table(b, 1).start()
    load_table(0).start()

    def ladder_piece(r, p):
        def piece():
            if r == 0:
                loads[p].wait()
            held = amps[r][mine, p]
            total = jnp.zeros((orbitals, orbitals), jnp.float32)
            for q in range(0, fitted, 2):
                one = factors[p, q]
                two = factors[p, q + 1]
                half = jnp.concatenate(
                    [contract(one, held, 1, 0), contract(two, held, 1, 0)], axis=1
                ).astype(jnp.bfloat16)
                total = total + contract(half, jnp.concatenate([one, two], axis=1), 1, 1)
            ladder[p] = total
        return piece

    def margins(b):
        for s in range(slots):
            margin[b, s] = contract(
                rows_basis[b][table[b, s, 0]], group_basis_flat(table[b, s, 1]), 0, 0
            ).astype(jnp.bfloat16)

    def group_basis_flat(q):
        return group_basis[lax.div(q, own_pairs), lax.rem(q, own_pairs)]

    def couple(r, b):
        lefts = []
        for s in range(slots):
            q = table[b, s, 1]
            block = amps[r][lax.div(q, own_pairs), lax.rem(q, own_pairs)]
            lefts.append((contract(margin[b, s], block, 1, 0) * floats_in[b, s : s + 1, :]).astype(jnp.bfloat16))
        total = jnp.zeros((orbitals, orbitals), jnp.float32)
        for s in range(slots):
            keep = floats_in[b, slots + s : slots + s + 1, :] > 0.0
            total = jnp.where(keep, total, 0.0) + contract(lefts[s], margin[b, s], 1, 1)
            sums[b, s] = total

    def partial(b, p):
        return sums[b, table[b, slots + p, 0]]

    def push_y(r, h, k):
        return pltpu.make_async_remote_copy(
            src_ref=to_y.at[r, h, span(k)], dst_ref=from_y.at[r, h, span(k)],
            send_sem=y_send, recv_sem=y_recv.at[r, h, k], device_id=(dev_y,), device_id_type=MESH,
        )

    def push_z(r, k):
        return pltpu.make_async_remote_copy(
            src_ref=to_z.at[r, span(k)], dst_ref=from_z.at[r, span(k)],
            send_sem=z_send, recv_sem=z_recv.at[r, k], device_id=(dev_h,), device_id_type=MESH,
        )

    def give_y(r, h):
        for k in range(pieces):
            for p in (2 * k, 2 * k + 1):
                to_y[r, h, p] = partial((3, 1)[h], p).astype(jnp.bfloat16)
            push_y(r, h, k).start()

    def give_z(r, k):
        push_y(r, 0, k).wait_recv()
        for p in (2 * k, 2 * k + 1):
            to_z[r, p] = (partial(2, p) + from_y[r, 0, p].astype(jnp.float32)).astype(jnp.bfloat16)
        push_z(r, k).start()

    def update(r, k):
        push_y(r, 1, k).wait_recv()
        push_z(r, k).wait_recv()
        for p in (2 * k, 2 * k + 1):
            total = partial(0, p) + from_y[r, 1, p].astype(jnp.float32) + from_z[r, p].astype(jnp.float32) + ladder[p]
            esum, divisor, driving = pair_terms(p)
            amplitudes = out_ref[p]
            residual = driving + esum * amplitudes + total
            amplitudes = amplitudes - residual / divisor
            out_ref[p] = amplitudes
            if r + 1 < ITERS:
                amps[r + 1][mine, p] = amplitudes.astype(jnp.bfloat16)
        if r + 1 < ITERS:
            own(r + 2, k)

    for b in range(QUAD):
        sums[b, slots] = jnp.zeros((orbitals, orbitals), jnp.float32)

    def gather_events(u):
        found = []
        for k in range(pieces + 1):
            if k < pieces:
                found += [came(u, 0, k), came(u, 1, k)]
            if k > 0:
                found.append(came(u, 2, k - 1))
        return found

    rows_in = []
    for k in range(pieces):
        rows_in += [row_came(2, k), row_came(1, k)]
        if k > 0:
            rows_in.append(row_came(3, k - 1))
    rows_in.append(row_came(3, pieces - 1))
    basis_in = gather_events(0)
    events = []
    for i in range(max(len(rows_in), len(basis_in))):
        events += basis_in[i : i + 1] + rows_in[i : i + 1]
    fill = [ladder_piece(0, p) for p in range(own_pairs)]
    done = 0
    for i, event in enumerate(events):
        event()
        upto = own_pairs * (i + 1) // len(events)
        for piece in fill[done:upto]:
            piece()
        done = upto
    for b in range(1, QUAD):
        push_table(b, 0).wait_recv()
        push_table(b, 1).wait_recv()
        load_table(b).start()
    sibling_done(0)
    for b in range(QUAD):
        load_table(b).wait()
    events = gather_events(1)
    for event in events[: len(events) // 4]:
        event()
    for b in (3, 2, 1, 0):
        margins(b)
        for event in events[len(events) * (4 - b) // 5 : len(events) * (5 - b) // 5] if False else ():
            event()
    for event in events[len(events) // 4 :]:
        event()
    sibling_done(1)

    for r in range(ITERS):
        couple(r, 3)
        give_y(r, 0)
        couple(r, 2)
        give_z(r, 0)
        give_z(r, 1)
        couple(r, 1)
        give_y(r, 1)
        for k in range(2, pieces):
            give_z(r, k)
        couple(r, 0)
        rest = [ladder_piece(r, p) for p in range(own_pairs)] if r > 0 else []
        ahead = 2 if r > 0 else 0
        rest = rest[ahead:]
        nxt = gather_events(r + 2) if r + 1 < ITERS else []
        for k in range(pieces):
            upto = max(0, 2 * (k + 1) - ahead)
            start = max(0, 2 * k - ahead)
            for piece in rest[start:upto]:
                piece()
            update(r, k)
            if nxt and k > 0:
                for event in nxt[3 * (k - 1) - (1 if k > 1 else 0) : 3 * k - 1]:
                    event()
        if nxt:
            left = nxt[3 * (pieces - 1) - 1 :]
            fill = [ladder_piece(r + 1, p) for p in range(2)]
            for i, event in enumerate(left):
                event()
                if i % 2 == 1 and fill:
                    fill.pop(0)()
            for piece in fill:
                piece()
            sibling_done(r + 2)

    for u in range(len(bufs)):
        sends_done(u)
    view = group_basis.at[pl.ds(0, 3)]
    pltpu.make_async_copy(view, view, basis_send).wait()
    for b in range(1, QUAD):
        push_table(b, 0).wait_send()
        push_table(b, 1).wait_send()
    pltpu.make_async_copy(to_y, to_y, y_send).wait()
    pltpu.make_async_copy(to_z, to_z, z_send).wait()


def fused(
    n, pno_basis, pno_count, partner_owner, partner_local, exchange_k, ladder_factor,
    pno_energy, occ_energy, coupling_fock,
):
    own_pairs, domain, orbitals = pno_basis.shape
    partners = partner_owner.shape[1]
    slots = GROUP * (-(-own_pairs * partners // n))
    pieces = own_pairs // 2
    smem = pl.BlockSpec(memory_space=pltpu.SMEM)
    vmem = pl.BlockSpec(memory_space=pltpu.VMEM)
    square = (orbitals, orbitals)
    amps = pltpu.VMEM((GROUP, own_pairs) + square, jnp.bfloat16)
    row = pltpu.VMEM((own_pairs, domain, orbitals), jnp.bfloat16)
    ints = pltpu.VMEM((QUAD, slots + own_pairs, 128), jnp.int32)
    floats = pltpu.VMEM((QUAD, 2 * slots, 128), jnp.float32)
    dma = pltpu.SemaphoreType.DMA
    return pl.pallas_call(
        functools.partial(kernel, slots),
        out_shape=jax.ShapeDtypeStruct((own_pairs, orbitals, orbitals), jnp.float32),
        in_specs=[vmem, smem, vmem, vmem, vmem, pl.BlockSpec(memory_space=pl.ANY), vmem, smem, vmem],
        out_specs=vmem,
        scratch_shapes=[
            pltpu.VMEM((GROUP, own_pairs, domain, orbitals), jnp.bfloat16),
            row, row, row, row,
            amps, amps, amps,
            pltpu.VMEM(ladder_factor.shape, jnp.bfloat16),
            pltpu.VMEM((QUAD, slots) + square, jnp.bfloat16),
            pltpu.VMEM((QUAD, slots + 1) + square, jnp.float32),
            pltpu.VMEM((own_pairs,) + square, jnp.float32),
            pltpu.VMEM((ITERS, 2, own_pairs) + square, jnp.bfloat16),
            pltpu.VMEM((ITERS, own_pairs) + square, jnp.bfloat16),
            pltpu.VMEM((ITERS, 2, own_pairs) + square, jnp.bfloat16),
            pltpu.VMEM((ITERS, own_pairs) + square, jnp.bfloat16),
            ints, ints, floats, floats,
            pltpu.SMEM((QUAD, slots + own_pairs, 128), jnp.int32),
            dma((own_pairs,)),
            dma((ITERS + 1, 3, pieces)),
            dma((ITERS + 1,)),
            dma((ITERS + 1,)),
            dma((QUAD, pieces)),
            dma,
            dma((2, QUAD)),
            dma((2, QUAD)),
            dma((QUAD,)),
            dma((ITERS, 2, pieces)),
            dma((ITERS, pieces)),
            dma,
            dma,
        ],
        compiler_params=pltpu.CompilerParams(
            collective_id=0, has_side_effects=True, vmem_limit_bytes=VMEM_BYTES
        ),
        name="jacobi",
    )(
        pno_basis, pno_count, partner_owner, partner_local, exchange_k, ladder_factor,
        pno_energy, occ_energy, coupling_fock,
    )


def shards(*args):
    n = lax.axis_size("pairs")
    own_pairs, domain, orbitals = args[0].shape
    fitted, partners = args[5].shape[1], args[2].shape[1]
    square = orbitals * orbitals
    each = -(-own_pairs * partners // n)
    slots = QUAD * GROUP * each
    held = 2 * own_pairs * orbitals * domain * (GROUP + QUAD + 2) + 2 * args[5].size
    held += square * (2 * ITERS * own_pairs * (GROUP + 6) + slots * 6 + own_pairs * 24)
    fits = held < VMEM_BYTES - (4 << 20)
    exact = n == QUAD * GROUP and own_pairs * partners == n * each
    if exact and own_pairs % 8 == 0 and fitted % 2 == 0 and fits:
        return fused(n, *args)
    return gathered_rows(*args)


def gathered_rows(
    pno_basis,
    pno_count,
    partner_owner,
    partner_local,
    exchange_k,
    ladder_factor,
    pno_energy,
    occ_energy,
    coupling_fock,
):
    own_pairs, domain, orbitals = pno_basis.shape
    fitted = ladder_factor.shape[1]
    partners = partner_owner.shape[1]
    listed = own_pairs * partners
    columns = lax.broadcasted_iota(jnp.int32, (own_pairs, orbitals), 1)
    live_cols = (columns < pno_count[:, None]).astype(jnp.float32)
    masked_basis = pno_basis * live_cols[:, None, :].astype(jnp.bfloat16)
    partner = (partner_owner * own_pairs + partner_local).reshape(listed)

    def rows_of(every):
        return lax.map(lambda i: lax.dynamic_index_in_dim(every, i, 0, keepdims=False), partner)

    every_basis = lax.all_gather(masked_basis, "pairs", axis=0, tiled=True)
    partner_basis = rows_of(every_basis).reshape(own_pairs, partners, domain, orbitals)
    margin = jnp.einsum(
        "rva,rcvb->rcab", masked_basis, partner_basis, preferred_element_type=jnp.float32
    ).astype(jnp.bfloat16)
    energy_sum = pno_energy[:, :, None] + pno_energy[:, None, :] - occ_energy[:, None, None]
    divisor = energy_sum + level_shift
    driving = exchange_k.astype(jnp.float32) * (live_cols[:, :, None] * live_cols[:, None, :])
    amplitudes = -driving / divisor
    weights = coupling_fock.astype(jnp.float32)
    group_width = 8
    for iteration in range(ITERS):
        sent_amps = amplitudes.astype(jnp.bfloat16)
        every_amps = lax.all_gather(sent_amps, "pairs", axis=0, tiled=True)

        def add_group(group_index, total):
            factors = lax.dynamic_slice_in_dim(
                ladder_factor, group_index * group_width, group_width, 1
            )
            ladder_half = jnp.einsum(
                "rqac,rcd->rqad", factors, sent_amps, preferred_element_type=jnp.float32
            ).astype(jnp.bfloat16)
            return total + jnp.einsum(
                "rqad,rqbd->rab", ladder_half, factors, preferred_element_type=jnp.float32
            )

        ladder = lax.fori_loop(
            0,
            fitted // group_width,
            add_group,
            jnp.zeros((own_pairs, orbitals, orbitals), jnp.float32),
        )
        partner_amps = rows_of(every_amps)
        partner_amps = partner_amps.reshape(own_pairs, partners, orbitals, orbitals)
        left_half = jnp.einsum(
            "rcab,rcbd->rcad", margin, partner_amps, preferred_element_type=jnp.float32
        )
        left_half = (left_half * weights[:, :, None, None]).astype(jnp.bfloat16)
        gathered_terms = jnp.einsum(
            "rcad,rced->rcae", left_half, margin, preferred_element_type=jnp.float32
        ).astype(jnp.bfloat16)
        coupled = jnp.sum(gathered_terms, axis=1, dtype=jnp.float32)
        residual = driving + energy_sum * amplitudes + coupled + ladder
        amplitudes = amplitudes - residual / divisor
    return amplitudes


def solution(mesh):
    return jax.shard_map(
        shards,
        mesh=mesh,
        in_specs=(
            P("pairs", None, None),
            P("pairs"),
            P("pairs", None),
            P("pairs", None),
            P("pairs", None, None),
            P("pairs", None, None, None),
            P("pairs", None),
            P("pairs"),
            P("pairs", None),
        ),
        out_specs=P("pairs", None, None),
        check_vma=False,
    )
```

```python
import functools
import jax
import jax.numpy as jnp
from jax import lax
from jax.experimental import pallas as pl
from jax.experimental.pallas import tpu as pltpu
from jax.sharding import PartitionSpec as P

ITERS = 3


level_shift = 0.3
VMEM_BYTES = 67043328
MESH = pl.DeviceIdType.MESH


def contract(a, b, da, db):
    return lax.dot_general(a, b, (((da,), (db,)), ((), ())), preferred_element_type=jnp.float32)


GROUP = 8
QUAD = 4


def cuts(own_pairs):
    twos = tuple((p, 2) for p in range(0, own_pairs, 2))
    inner = tuple((p, 2) for p in range(2, own_pairs // 2, 2))
    ending = tuple((p, 1) for p in range(own_pairs // 2, own_pairs))
    return twos, ((0, 1), (1, 1)) + inner + ending


def table_rows(slots, own_pairs, ref_owner, ref_local, ref_fock, here):
    owner = ref_owner[...]
    local = ref_local[...]
    fock = ref_fock[...].astype(jnp.float32)
    partners = owner.shape[1]
    lane = lax.broadcasted_iota(jnp.int32, owner.shape, 1)
    row = lax.broadcasted_iota(jnp.int32, owner.shape, 0)
    high = lax.shift_right_logical(owner, 4)
    mid = lax.shift_right_logical(owner, 2) & 1
    place = ((lax.shift_right_logical(owner, 3) & 1) * 4 + (owner & 3)) * own_pairs + local
    slot = lax.broadcasted_iota(jnp.int32, (slots, partners), 0)
    slot_wide = lax.broadcasted_iota(jnp.int32, (slots, 128), 0)
    lane_wide = lax.broadcasted_iota(jnp.int32, (slots, 128), 1)
    my_high, my_mid = here
    found = []
    for b in range(QUAD):
        want_high = my_high if b < 2 else 1 - my_high
        want_mid = my_mid if b % 2 == 0 else 1 - my_mid
        chosen = (high == want_high) & (mid == want_mid)
        ones = jnp.where(chosen, 1, 0)
        before = jnp.zeros_like(ones)
        number = jnp.zeros((own_pairs, 1), jnp.int32)
        for c in range(partners):
            before = before + jnp.where(lane > c, ones[:, c : c + 1], 0)
            number = number + ones[:, c : c + 1]
        ahead = jnp.zeros((own_pairs, partners), jnp.int32)
        wide = jnp.broadcast_to(number, (own_pairs, partners))
        for p in range(own_pairs):
            ahead = ahead + jnp.where(row > p, wide[p : p + 1, :], 0)
        rank = jnp.where(chosen, before + ahead, -1)
        pair = jnp.zeros((slots, partners), jnp.int32)
        other = jnp.zeros((slots, partners), jnp.int32)
        weight = jnp.zeros((slots, partners), jnp.float32)
        begins = jnp.zeros((slots, partners), jnp.float32)
        for p in range(own_pairs):
            hit = rank[p : p + 1, :] == slot
            pair = pair + jnp.where(hit, p, 0)
            other = other + jnp.where(hit, place[p : p + 1, :], 0)
            weight = weight + jnp.where(hit, fock[p : p + 1, :], 0.0)
            begins = jnp.where(ahead[p : p + 1, :] == slot, 1.0, begins)
        sums = [jnp.zeros((slots, 1), v.dtype) for v in (pair, other, weight)]
        for c in range(partners):
            sums = [t + v[:, c : c + 1] for t, v in zip(sums, (pair, other, weight))]
        ints = jnp.where(lane_wide == 0, jnp.broadcast_to(sums[0], (slots, 128)), jnp.broadcast_to(sums[1], (slots, 128)))
        last = jnp.where(number > 0, jnp.minimum(ahead[:, 0:1] + number - 1, slots), slots)
        found.append((
            ints,
            jnp.broadcast_to(last, (own_pairs, 128)),
            jnp.broadcast_to(sums[2], (slots, 128)),
            jnp.broadcast_to(1.0 - begins[:, 0:1], (slots, 128)),
        ))
    return found


def kernel(
    slots, basis_ref, count_ref, owner_ref, local_ref, exchange_ref, ladder_hbm, energy_ref,
    occ_ref, fock_ref, out_ref,
    group_basis, row_own, row_y, row_z, row_yz, amps_a, amps_b, amps_c, factors, margin, sums, ladder,
    from_y, from_z, to_y, to_z, ints_out, ints_in, floats_out, floats_in, table,
    load_sem, recv_sem, recv_sib, send_sem, basis_recv, basis_send, table_recv, table_send, table_load,
    y_recv, z_recv, y_send, z_send,
):
    own_pairs, domain, orbitals = basis_ref.shape
    fitted = factors.shape[1]
    me = lax.axis_index("pairs")
    core = me % 2
    bit_x = me // 2 % 2
    bit_y = me // 4 % 2
    bit_l = me // 8 % 2
    bit_h = me // 16
    sibling = me + 1 - 2 * core
    dev_x = me + 2 * (1 - 2 * bit_x)
    dev_y = me + 4 * (1 - 2 * bit_y)
    dev_l = me + 8 * (1 - 2 * bit_l)
    dev_h = me + 16 * (1 - 2 * bit_h)
    dev_d = dev_l + 2 * (1 - 2 * bit_x)
    dev_yh = dev_h + 4 * (1 - 2 * bit_y)
    mine = bit_l * 4 + bit_x * 2 + core
    mine_x = bit_l * 4 + (1 - bit_x) * 2 + core
    mine_l = (1 - bit_l) * 4 + bit_x * 2 + core
    mine_d = (1 - bit_l) * 4 + (1 - bit_x) * 2 + core
    rows_basis = (row_own, row_y, row_z, row_yz)
    bufs = (group_basis, amps_a, amps_b, amps_c)
    amps = (amps_a, amps_b, amps_c)
    twos, ends = cuts(own_pairs)
    cut = (twos, twos, ends, ends)
    ways = [["z"] * len(c) for c in cut]
    for k in range(len(twos) // 2, len(twos)):
        ways[1][k] = "x"
    for u in (2, 3):
        ways[u][-2:] = ["routed", "routed"]

    loads = [
        pltpu.make_async_copy(ladder_hbm.at[p], factors.at[p], load_sem.at[p])
        for p in range(own_pairs)
    ]

    def pairs_of(c, k):
        lo, cnt = c[k]
        return range(lo, lo + cnt)

    def push(u, k, owner, dev, sem):
        view = bufs[u].at[owner, pl.ds(*cut[u][k])]
        return pltpu.make_async_remote_copy(
            src_ref=view, dst_ref=view, send_sem=send_sem.at[u], recv_sem=sem,
            device_id=(dev,), device_id_type=MESH,
        )

    def own_z(u, k):
        push(u, k, mine, dev_l, recv_sem.at[u, 1, k]).start()

    def own_x(u, k):
        push(u, k, mine, dev_x, recv_sem.at[u, 0, k]).start()

    def own(u, k):
        own_z(u, k)
        own_x(u, k)
        if ways[u][k] == "routed":
            push(u, k, mine, dev_d, recv_sem.at[u, 2, k]).start()
        own_sibling(u, k)

    def own_sibling(u, k):
        push(u, k, mine, sibling, recv_sib.at[u]).start()

    def came(u, kind, k):
        def go():
            owner = (mine_x, mine_l, mine_d)[kind]
            push(u, k, owner, sibling, recv_sem.at[u, kind, k]).wait_recv()
            if kind == 0 and ways[u][k] == "x":
                push(u, k, owner, dev_l, recv_sem.at[u, 2, k]).start()
            if kind == 1 and ways[u][k] == "z":
                push(u, k, owner, dev_x, recv_sem.at[u, 2, k]).start()
            push(u, k, owner, sibling, recv_sib.at[u]).start()
        return go

    def sibling_done(u):
        view = bufs[u].at[pl.ds(0, GROUP // 2)]
        pltpu.make_async_copy(view, view, recv_sib.at[u]).wait()

    def sends_done(u):
        view = bufs[u].at[pl.ds(0, GROUP - 1)]
        pltpu.make_async_copy(view, view, send_sem.at[u]).wait()

    def push_row(src, b, k, dev):
        return pltpu.make_async_remote_copy(
            src_ref=src.at[pl.ds(*twos[k])], dst_ref=rows_basis[b].at[pl.ds(*twos[k])],
            send_sem=basis_send, recv_sem=basis_recv.at[b, k],
            device_id=(dev,), device_id_type=MESH,
        )

    def row_came(b, k):
        def go():
            push_row(row_own, b, k, dev_y).wait_recv()
            if b == 2:
                push_row(row_z, 3, k, dev_y).start()
        return go

    lanes = lax.broadcasted_iota(jnp.int32, (orbitals, orbitals), 1)
    rows = lax.broadcasted_iota(jnp.int32, (orbitals, orbitals), 0)
    energy_cols = jnp.transpose(energy_ref[...])

    def pair_terms(p):
        esum = energy_cols[:, p : p + 1] + energy_ref[p : p + 1, :] - occ_ref[p]
        count = count_ref[p]
        live = (lanes < count) & (rows < count)
        driving = jnp.where(live, exchange_ref[p].astype(jnp.float32), 0.0)
        return esum, esum + level_shift, driving

    barrier = pltpu.get_barrier_semaphore()
    near = (sibling, dev_x, dev_l, dev_d, dev_y, dev_h, dev_yh)
    for dev in near:
        pl.semaphore_signal(barrier, inc=1, device_id=(dev,), device_id_type=MESH)
    for load in loads:
        load.start()

    basis_lanes = lax.broadcasted_iota(jnp.int32, (domain, orbitals), 1)

    def mask_basis(p):
        held = jnp.where(
            basis_lanes < count_ref[p], basis_ref[p].astype(jnp.float32), 0.0
        ).astype(jnp.bfloat16)
        group_basis[mine, p] = held
        row_own[p] = held

    def first_amps(p):
        esum, divisor, driving = pair_terms(p)
        first = -driving / divisor
        out_ref[p] = first
        amps_a[mine, p] = first.astype(jnp.bfloat16)

    for p in range(own_pairs):
        mask_basis(p)
    pl.semaphore_wait(barrier, len(near))

    for k in range(len(twos)):
        own(0, k)
        push_row(row_own, 1, k, dev_y).start()
    for k in range(len(twos)):
        push_row(row_own, 2, k, dev_h).start()

    for p in range(own_pairs):
        first_amps(p)
    for k in range(len(twos)):
        own_z(1, k)
        own_sibling(1, k)

    found = table_rows(slots, own_pairs, owner_ref, local_ref, fock_ref, (bit_h, bit_y))
    for b in range(QUAD):
        ints, last, weight, keep = found[b]
        to_int, to_float = (ints_in, floats_in) if b == 0 else (ints_out, floats_out)
        to_int[b, 0:slots] = ints
        to_int[b, slots : slots + own_pairs] = last
        to_float[b, 0:slots] = weight
        to_float[b, slots : 2 * slots] = keep

    def push_table(b, which):
        src, dst = ((ints_out, ints_in), (floats_out, floats_in))[which]
        return pltpu.make_async_remote_copy(
            src_ref=src.at[b], dst_ref=dst.at[b], send_sem=table_send.at[which, b], recv_sem=table_recv.at[which, b],
            device_id=((dev_y, dev_y, dev_h, dev_yh)[b],), device_id_type=MESH,
        )

    def load_table(b):
        return pltpu.make_async_copy(ints_in.at[b], table.at[b], table_load.at[b])

    for b in range(1, QUAD):
        push_table(b, 0).start()
        push_table(b, 1).start()
    load_table(0).start()

    def ladder_piece(r, p):
        def piece():
            if r == 0:
                loads[p].wait()
            held = amps[r][mine, p]
            total = jnp.zeros((orbitals, orbitals), jnp.float32)
            for q in range(0, fitted, 2):
                one = factors[p, q]
                two = factors[p, q + 1]
                half = jnp.concatenate(
                    [contract(one, held, 1, 0), contract(two, held, 1, 0)], axis=1
                ).astype(jnp.bfloat16)
                total = total + contract(half, jnp.concatenate([one, two], axis=1), 1, 1)
            ladder[p] = total
        return piece

    def margins(b):
        for s in range(slots):
            margin[b, s] = contract(
                rows_basis[b][table[b, s, 0]], group_basis_flat(table[b, s, 1]), 0, 0
            ).astype(jnp.bfloat16)

    def group_basis_flat(q):
        return group_basis[lax.div(q, own_pairs), lax.rem(q, own_pairs)]

    def couple(r, b):
        lefts = []
        for s in range(slots):
            q = table[b, s, 1]
            block = amps[r][lax.div(q, own_pairs), lax.rem(q, own_pairs)]
            lefts.append((contract(margin[b, s], block, 1, 0) * floats_in[b, s : s + 1, :]).astype(jnp.bfloat16))
        total = jnp.zeros((orbitals, orbitals), jnp.float32)
        for s in range(slots):
            keep = floats_in[b, slots + s : slots + s + 1, :] > 0.0
            total = jnp.where(keep, total, 0.0) + contract(lefts[s], margin[b, s], 1, 1)
            sums[b, s] = total

    def partial(b, p):
        return sums[b, table[b, slots + p, 0]]

    def push_y(r, h, k):
        return pltpu.make_async_remote_copy(
            src_ref=to_y.at[r, h, pl.ds(*ends[k])], dst_ref=from_y.at[r, h, pl.ds(*ends[k])],
            send_sem=y_send, recv_sem=y_recv.at[r, h, k],
            device_id=(dev_yh if (h, k) == (0, 0) else dev_y,), device_id_type=MESH,
        )

    def push_z(r, k):
        return pltpu.make_async_remote_copy(
            src_ref=to_z.at[r, pl.ds(*ends[k])], dst_ref=from_z.at[r, pl.ds(*ends[k])],
            send_sem=z_send, recv_sem=z_recv.at[r, k], device_id=(dev_h,), device_id_type=MESH,
        )

    def give_y(r, h, k):
        for p in pairs_of(ends, k):
            to_y[r, h, p] = partial((3, 1)[h], p).astype(jnp.bfloat16)
        push_y(r, h, k).start()

    def give_z(r, k):
        if k > 0:
            push_y(r, 0, k).wait_recv()
        for p in pairs_of(ends, k):
            total = partial(2, p)
            if k > 0:
                total = total + from_y[r, 0, p].astype(jnp.float32)
            to_z[r, p] = total.astype(jnp.bfloat16)
        push_z(r, k).start()

    def update(r, k):
        push_y(r, 1, k).wait_recv()
        push_z(r, k).wait_recv()
        if k == 0:
            push_y(r, 0, k).wait_recv()
        for p in pairs_of(ends, k):
            total = partial(0, p) + from_y[r, 1, p].astype(jnp.float32) + from_z[r, p].astype(jnp.float32) + ladder[p]
            if k == 0:
                total = total + from_y[r, 0, p].astype(jnp.float32)
            esum, divisor, driving = pair_terms(p)
            amplitudes = out_ref[p]
            residual = driving + esum * amplitudes + total
            amplitudes = amplitudes - residual / divisor
            out_ref[p] = amplitudes
            if r + 1 < ITERS:
                amps[r + 1][mine, p] = amplitudes.astype(jnp.bfloat16)
        if r + 1 < ITERS:
            own(r + 2, k)

    for b in range(QUAD):
        sums[b, slots] = jnp.zeros((orbitals, orbitals), jnp.float32)

    def bx(k):
        return came(0, 0, k)

    def bz(k):
        return came(0, 1, k)

    def by(k):
        return row_came(1, k)

    def bh(k):
        return row_came(2, k)

    def fill(p):
        return ladder_piece(0, p)

    def ax(k):
        return came(1, 0, k)

    def az(k):
        return came(1, 1, k)

    def tables_in():
        for b in range(1, QUAD):
            push_table(b, 0).wait_recv()
            push_table(b, 1).wait_recv()
            load_table(b).start()

    number = len(twos)
    fills = [fill(p) for p in range(own_pairs)]
    each = -(-own_pairs // number)
    later = [*range(number // 2, number), *range(number // 2)]
    todo = []
    for k in range(number):
        if k == number - 1:
            todo += [bh(j) for j in range(number // 2)]
        todo += fills[k * each : (k + 1) * each] + [bx(k), bz(k), by(k)]
        if number // 2 - 1 <= k < number - 1:
            first = (k + 1 - number // 2) * 2
            todo += [lambda j=j: own_x(1, j) for j in later[first : first + 2]]
    todo += [tables_in]
    for k in range(number):
        todo += [bh(k)] if k >= number // 2 else []
        todo += [came(0, 2, k)]
    for i in range(number):
        todo += [az(i), ax(later[i])]
        if i == number // 2 - 1:
            todo += [lambda: sibling_done(0)] + [load_table(b).wait for b in range(QUAD)] + [lambda: margins(0)]
    todo += [lambda: margins(1), lambda: margins(2)]
    todo += [row_came(3, k) for k in range(number)] + [lambda: margins(3)]
    todo += [came(1, 2, k) for k in later]
    for event in todo:
        event()
    sibling_done(1)

    number = len(ends)
    early = 2
    for r in range(ITERS):
        rest = [ladder_piece(r, p) for p in range(early, own_pairs)] if r > 0 else []
        more = r + 1 < ITERS

        def ladders(upto):
            while rest and own_pairs - len(rest) < upto:
                rest.pop(0)()

        def both(k):
            if more and k >= 0:
                came(r + 2, 1, k)()
                came(r + 2, 0, k)()

        def diag(k):
            if more and k >= 0:
                came(r + 2, 2, k)()

        couple(r, 3)
        for k in range(4):
            give_y(r, 0, k)
        couple(r, 2)
        give_z(r, 0)
        couple(r, 1)
        give_y(r, 1, 0)
        give_y(r, 0, 4)
        give_y(r, 1, 1)
        give_z(r, 1)
        for k in range(5, number):
            give_y(r, 1, k - 3)
            give_y(r, 0, k)
        for k in range(number - 3, number):
            give_y(r, 1, k)
        couple(r, 0)
        give_z(r, 2)
        ladders(early + 1)
        given = 3
        for k in range(number):
            lo, cnt = ends[k]
            ladders(lo + cnt)
            update(r, k)
            upto = min(number, k + 4 + (k > 0))
            for j in range(given, upto):
                give_z(r, j)
            given = upto
            ladders(early + 2 + k)
            both(k - 2)
            diag(k - 4)
        if more:
            ladder_piece(r + 1, 0)()
            diag(number - 4)
            both(number - 2)
            ladder_piece(r + 1, 1)()
            diag(number - 3)
            diag(number - 2)
            both(number - 1)
            diag(number - 1)
            sibling_done(r + 2)

    for u in range(len(bufs)):
        sends_done(u)
    view = group_basis.at[pl.ds(0, 3)]
    pltpu.make_async_copy(view, view, basis_send).wait()
    for b in range(1, QUAD):
        push_table(b, 0).wait_send()
        push_table(b, 1).wait_send()
    pltpu.make_async_copy(to_y, to_y, y_send).wait()
    pltpu.make_async_copy(to_z, to_z, z_send).wait()


def fused(
    n, pno_basis, pno_count, partner_owner, partner_local, exchange_k, ladder_factor,
    pno_energy, occ_energy, coupling_fock,
):
    own_pairs, domain, orbitals = pno_basis.shape
    partners = partner_owner.shape[1]
    slots = GROUP * (-(-own_pairs * partners // n))
    pieces = max(len(c) for c in cuts(own_pairs))
    smem = pl.BlockSpec(memory_space=pltpu.SMEM)
    vmem = pl.BlockSpec(memory_space=pltpu.VMEM)
    square = (orbitals, orbitals)
    amps = pltpu.VMEM((GROUP, own_pairs) + square, jnp.bfloat16)
    row = pltpu.VMEM((own_pairs, domain, orbitals), jnp.bfloat16)
    ints = pltpu.VMEM((QUAD, slots + own_pairs, 128), jnp.int32)
    floats = pltpu.VMEM((QUAD, 2 * slots, 128), jnp.float32)
    dma = pltpu.SemaphoreType.DMA
    return pl.pallas_call(
        functools.partial(kernel, slots),
        out_shape=jax.ShapeDtypeStruct((own_pairs, orbitals, orbitals), jnp.float32),
        in_specs=[vmem, smem, vmem, vmem, vmem, pl.BlockSpec(memory_space=pl.ANY), vmem, smem, vmem],
        out_specs=vmem,
        scratch_shapes=[
            pltpu.VMEM((GROUP, own_pairs, domain, orbitals), jnp.bfloat16),
            row, row, row, row,
            amps, amps, amps,
            pltpu.VMEM(ladder_factor.shape, jnp.bfloat16),
            pltpu.VMEM((QUAD, slots) + square, jnp.bfloat16),
            pltpu.VMEM((QUAD, slots + 1) + square, jnp.float32),
            pltpu.VMEM((own_pairs,) + square, jnp.float32),
            pltpu.VMEM((ITERS, 2, own_pairs) + square, jnp.bfloat16),
            pltpu.VMEM((ITERS, own_pairs) + square, jnp.bfloat16),
            pltpu.VMEM((ITERS, 2, own_pairs) + square, jnp.bfloat16),
            pltpu.VMEM((ITERS, own_pairs) + square, jnp.bfloat16),
            ints, ints, floats, floats,
            pltpu.SMEM((QUAD, slots + own_pairs, 128), jnp.int32),
            dma((own_pairs,)),
            dma((ITERS + 1, 3, pieces)),
            dma((ITERS + 1,)),
            dma((ITERS + 1,)),
            dma((QUAD, pieces)),
            dma,
            dma((2, QUAD)),
            dma((2, QUAD)),
            dma((QUAD,)),
            dma((ITERS, 2, pieces)),
            dma((ITERS, pieces)),
            dma,
            dma,
        ],
        compiler_params=pltpu.CompilerParams(
            collective_id=0, has_side_effects=True, vmem_limit_bytes=VMEM_BYTES
        ),
        name="jacobi",
    )(
        pno_basis, pno_count, partner_owner, partner_local, exchange_k, ladder_factor,
        pno_energy, occ_energy, coupling_fock,
    )


def shards(*args):
    n = lax.axis_size("pairs")
    own_pairs, domain, orbitals = args[0].shape
    fitted, partners = args[5].shape[1], args[2].shape[1]
    square = orbitals * orbitals
    each = -(-own_pairs * partners // n)
    slots = QUAD * GROUP * each
    held = 2 * own_pairs * orbitals * domain * (GROUP + QUAD + 2) + 2 * args[5].size
    held += square * (2 * ITERS * own_pairs * (GROUP + 6) + slots * 6 + own_pairs * 24)
    fits = held < VMEM_BYTES - (4 << 20)
    exact = n == QUAD * GROUP and own_pairs * partners == n * each
    if exact and own_pairs % 8 == 0 and fitted % 2 == 0 and fits:
        return fused(n, *args)
    return gathered_rows(*args)


def gathered_rows(
    pno_basis,
    pno_count,
    partner_owner,
    partner_local,
    exchange_k,
    ladder_factor,
    pno_energy,
    occ_energy,
    coupling_fock,
):
    own_pairs, domain, orbitals = pno_basis.shape
    fitted = ladder_factor.shape[1]
    partners = partner_owner.shape[1]
    listed = own_pairs * partners
    columns = lax.broadcasted_iota(jnp.int32, (own_pairs, orbitals), 1)
    live_cols = (columns < pno_count[:, None]).astype(jnp.float32)
    masked_basis = pno_basis * live_cols[:, None, :].astype(jnp.bfloat16)
    partner = (partner_owner * own_pairs + partner_local).reshape(listed)

    def rows_of(every):
        return lax.map(lambda i: lax.dynamic_index_in_dim(every, i, 0, keepdims=False), partner)

    every_basis = lax.all_gather(masked_basis, "pairs", axis=0, tiled=True)
    partner_basis = rows_of(every_basis).reshape(own_pairs, partners, domain, orbitals)
    margin = jnp.einsum(
        "rva,rcvb->rcab", masked_basis, partner_basis, preferred_element_type=jnp.float32
    ).astype(jnp.bfloat16)
    energy_sum = pno_energy[:, :, None] + pno_energy[:, None, :] - occ_energy[:, None, None]
    divisor = energy_sum + level_shift
    driving = exchange_k.astype(jnp.float32) * (live_cols[:, :, None] * live_cols[:, None, :])
    amplitudes = -driving / divisor
    weights = coupling_fock.astype(jnp.float32)
    group_width = 8
    for iteration in range(ITERS):
        sent_amps = amplitudes.astype(jnp.bfloat16)
        every_amps = lax.all_gather(sent_amps, "pairs", axis=0, tiled=True)

        def add_group(group_index, total):
            factors = lax.dynamic_slice_in_dim(
                ladder_factor, group_index * group_width, group_width, 1
            )
            ladder_half = jnp.einsum(
                "rqac,rcd->rqad", factors, sent_amps, preferred_element_type=jnp.float32
            ).astype(jnp.bfloat16)
            return total + jnp.einsum(
                "rqad,rqbd->rab", ladder_half, factors, preferred_element_type=jnp.float32
            )

        ladder = lax.fori_loop(
            0,
            fitted // group_width,
            add_group,
            jnp.zeros((own_pairs, orbitals, orbitals), jnp.float32),
        )
        partner_amps = rows_of(every_amps)
        partner_amps = partner_amps.reshape(own_pairs, partners, orbitals, orbitals)
        left_half = jnp.einsum(
            "rcab,rcbd->rcad", margin, partner_amps, preferred_element_type=jnp.float32
        )
        left_half = (left_half * weights[:, :, None, None]).astype(jnp.bfloat16)
        gathered_terms = jnp.einsum(
            "rcad,rced->rcae", left_half, margin, preferred_element_type=jnp.float32
        ).astype(jnp.bfloat16)
        coupled = jnp.sum(gathered_terms, axis=1, dtype=jnp.float32)
        residual = driving + energy_sum * amplitudes + coupled + ladder
        amplitudes = amplitudes - residual / divisor
    return amplitudes


def solution(mesh):
    return jax.shard_map(
        shards,
        mesh=mesh,
        in_specs=(
            P("pairs", None, None),
            P("pairs"),
            P("pairs", None),
            P("pairs", None),
            P("pairs", None, None),
            P("pairs", None, None, None),
            P("pairs", None),
            P("pairs"),
            P("pairs", None),
        ),
        out_specs=P("pairs", None, None),
        check_vma=False,
    )
```

```python
import functools
import jax
import jax.numpy as jnp
from jax import lax
from jax.experimental import pallas as pl
from jax.experimental.pallas import tpu as pltpu
from jax.sharding import PartitionSpec as P

ITERS = 3


level_shift = 0.3
VMEM_BYTES = 67043328
MESH = pl.DeviceIdType.MESH


def contract(a, b, da, db):
    return lax.dot_general(a, b, (((da,), (db,)), ((), ())), preferred_element_type=jnp.float32)


GROUP = 8
QUAD = 4


def cuts(own_pairs):
    twos = tuple((p, 2) for p in range(0, own_pairs, 2))
    inner = tuple((p, 2) for p in range(2, own_pairs // 2, 2))
    ending = tuple((p, 1) for p in range(own_pairs // 2, own_pairs))
    return twos, ((0, 1), (1, 1)) + inner + ending


def table_rows(slots, own_pairs, ref_owner, ref_local, ref_fock, here):
    owner = ref_owner[...]
    local = ref_local[...]
    fock = ref_fock[...].astype(jnp.float32)
    partners = owner.shape[1]
    lane = lax.broadcasted_iota(jnp.int32, owner.shape, 1)
    row = lax.broadcasted_iota(jnp.int32, owner.shape, 0)
    high = lax.shift_right_logical(owner, 4)
    mid = lax.shift_right_logical(owner, 2) & 1
    place = ((lax.shift_right_logical(owner, 3) & 1) * 4 + (owner & 3)) * own_pairs + local
    slot = lax.broadcasted_iota(jnp.int32, (slots, partners), 0)
    slot_wide = lax.broadcasted_iota(jnp.int32, (slots, 128), 0)
    lane_wide = lax.broadcasted_iota(jnp.int32, (slots, 128), 1)
    my_high, my_mid = here
    found = []
    for b in range(QUAD):
        want_high = my_high if b < 2 else 1 - my_high
        want_mid = my_mid if b % 2 == 0 else 1 - my_mid
        chosen = (high == want_high) & (mid == want_mid)
        ones = jnp.where(chosen, 1, 0)
        before = jnp.zeros_like(ones)
        number = jnp.zeros((own_pairs, 1), jnp.int32)
        for c in range(partners):
            before = before + jnp.where(lane > c, ones[:, c : c + 1], 0)
            number = number + ones[:, c : c + 1]
        ahead = jnp.zeros((own_pairs, partners), jnp.int32)
        wide = jnp.broadcast_to(number, (own_pairs, partners))
        for p in range(own_pairs):
            ahead = ahead + jnp.where(row > p, wide[p : p + 1, :], 0)
        rank = jnp.where(chosen, before + ahead, -1)
        pair = jnp.zeros((slots, partners), jnp.int32)
        other = jnp.zeros((slots, partners), jnp.int32)
        weight = jnp.zeros((slots, partners), jnp.float32)
        begins = jnp.zeros((slots, partners), jnp.float32)
        for p in range(own_pairs):
            hit = rank[p : p + 1, :] == slot
            pair = pair + jnp.where(hit, p, 0)
            other = other + jnp.where(hit, place[p : p + 1, :], 0)
            weight = weight + jnp.where(hit, fock[p : p + 1, :], 0.0)
            begins = jnp.where(ahead[p : p + 1, :] == slot, 1.0, begins)
        sums = [jnp.zeros((slots, 1), v.dtype) for v in (pair, other, weight)]
        for c in range(partners):
            sums = [t + v[:, c : c + 1] for t, v in zip(sums, (pair, other, weight))]
        ints = jnp.where(lane_wide == 0, jnp.broadcast_to(sums[0], (slots, 128)), jnp.broadcast_to(sums[1], (slots, 128)))
        last = jnp.where(number > 0, jnp.minimum(ahead[:, 0:1] + number - 1, slots), slots)
        found.append((
            ints,
            jnp.broadcast_to(last, (own_pairs, 128)),
            jnp.broadcast_to(sums[2], (slots, 128)),
            jnp.broadcast_to(1.0 - begins[:, 0:1], (slots, 128)),
        ))
    return found


def kernel(
    slots, basis_ref, count_ref, owner_ref, local_ref, exchange_ref, ladder_hbm, energy_ref,
    occ_ref, fock_ref, out_ref,
    group_basis, row_own, row_y, row_z, row_yz, amps_a, amps_b, amps_c, factors, margin, sums, ladder,
    from_y, from_z, to_y, to_z, ints_out, ints_in, floats_out, floats_in, table,
    load_sem, recv_sem, recv_sib, send_sem, basis_recv, basis_send, table_recv, table_send, table_load,
    y_recv, z_recv, y_send, z_send,
):
    own_pairs, domain, orbitals = basis_ref.shape
    fitted = factors.shape[1]
    me = lax.axis_index("pairs")
    core = me % 2
    bit_x = me // 2 % 2
    bit_y = me // 4 % 2
    bit_l = me // 8 % 2
    bit_h = me // 16
    sibling = me + 1 - 2 * core
    dev_x = me + 2 * (1 - 2 * bit_x)
    dev_y = me + 4 * (1 - 2 * bit_y)
    dev_l = me + 8 * (1 - 2 * bit_l)
    dev_h = me + 16 * (1 - 2 * bit_h)
    dev_d = dev_l + 2 * (1 - 2 * bit_x)
    dev_yh = dev_h + 4 * (1 - 2 * bit_y)
    mine = bit_l * 4 + bit_x * 2 + core
    mine_x = bit_l * 4 + (1 - bit_x) * 2 + core
    mine_l = (1 - bit_l) * 4 + bit_x * 2 + core
    mine_d = (1 - bit_l) * 4 + (1 - bit_x) * 2 + core
    rows_basis = (row_own, row_y, row_z, row_yz)
    bufs = (group_basis, amps_a, amps_b, amps_c)
    amps = (amps_a, amps_b, amps_c)
    twos, ends = cuts(own_pairs)
    cut = (twos, twos, ends, ends)
    ways = [["z"] * len(c) for c in cut]
    for k in range(len(twos) // 2, len(twos)):
        ways[1][k] = "x"
    for u in (2, 3):
        ways[u][-2:] = ["routed", "routed"]

    loads = [
        pltpu.make_async_copy(ladder_hbm.at[p], factors.at[p], load_sem.at[p])
        for p in range(own_pairs)
    ]

    def pairs_of(c, k):
        lo, cnt = c[k]
        return range(lo, lo + cnt)

    def push(u, k, owner, dev, sem):
        view = bufs[u].at[owner, pl.ds(*cut[u][k])]
        return pltpu.make_async_remote_copy(
            src_ref=view, dst_ref=view, send_sem=send_sem.at[u], recv_sem=sem,
            device_id=(dev,), device_id_type=MESH,
        )

    def own_z(u, k):
        push(u, k, mine, dev_l, recv_sem.at[u, 1, k]).start()

    def own_x(u, k):
        push(u, k, mine, dev_x, recv_sem.at[u, 0, k]).start()

    def own(u, k):
        own_z(u, k)
        own_x(u, k)
        if ways[u][k] == "routed":
            push(u, k, mine, dev_d, recv_sem.at[u, 2, k]).start()
        own_sibling(u, k)

    def own_sibling(u, k):
        push(u, k, mine, sibling, recv_sib.at[u]).start()

    def came(u, kind, k):
        def go():
            owner = (mine_x, mine_l, mine_d)[kind]
            push(u, k, owner, sibling, recv_sem.at[u, kind, k]).wait_recv()
            if kind == 0 and ways[u][k] == "x":
                push(u, k, owner, dev_l, recv_sem.at[u, 2, k]).start()
            if kind == 1 and ways[u][k] == "z":
                push(u, k, owner, dev_x, recv_sem.at[u, 2, k]).start()
            push(u, k, owner, sibling, recv_sib.at[u]).start()
        return go

    def sibling_done(u):
        view = bufs[u].at[pl.ds(0, GROUP // 2)]
        pltpu.make_async_copy(view, view, recv_sib.at[u]).wait()

    def sends_done(u):
        view = bufs[u].at[pl.ds(0, GROUP - 1)]
        pltpu.make_async_copy(view, view, send_sem.at[u]).wait()

    def push_row(src, b, k, dev):
        return pltpu.make_async_remote_copy(
            src_ref=src.at[pl.ds(*twos[k])], dst_ref=rows_basis[b].at[pl.ds(*twos[k])],
            send_sem=basis_send, recv_sem=basis_recv.at[b, k],
            device_id=(dev,), device_id_type=MESH,
        )

    def row_came(b, k):
        def go():
            push_row(row_own, b, k, dev_y).wait_recv()
            if b == 2:
                push_row(row_z, 3, k, dev_y).start()
        return go

    lanes = lax.broadcasted_iota(jnp.int32, (orbitals, orbitals), 1)
    rows = lax.broadcasted_iota(jnp.int32, (orbitals, orbitals), 0)
    energy_cols = jnp.transpose(energy_ref[...])

    def pair_terms(p):
        esum = energy_cols[:, p : p + 1] + energy_ref[p : p + 1, :] - occ_ref[p]
        count = count_ref[p]
        live = (lanes < count) & (rows < count)
        driving = jnp.where(live, exchange_ref[p].astype(jnp.float32), 0.0)
        return esum, esum + level_shift, driving

    barrier = pltpu.get_barrier_semaphore()
    near = (sibling, dev_x, dev_l, dev_d, dev_y, dev_h, dev_yh)
    for dev in near:
        pl.semaphore_signal(barrier, inc=1, device_id=(dev,), device_id_type=MESH)
    for load in loads:
        load.start()

    basis_lanes = lax.broadcasted_iota(jnp.int32, (domain, orbitals), 1)

    def mask_basis(p):
        held = jnp.where(
            basis_lanes < count_ref[p], basis_ref[p].astype(jnp.float32), 0.0
        ).astype(jnp.bfloat16)
        group_basis[mine, p] = held
        row_own[p] = held

    def first_amps(p):
        esum, divisor, driving = pair_terms(p)
        first = -driving / divisor
        out_ref[p] = first
        amps_a[mine, p] = first.astype(jnp.bfloat16)

    for p in range(own_pairs):
        mask_basis(p)
    pl.semaphore_wait(barrier, len(near))

    for k in range(len(twos)):
        own(0, k)
        push_row(row_own, 1, k, dev_y).start()
        if k >= 1:
            push_row(row_own, 2, k - 1, dev_h).start()
    push_row(row_own, 2, len(twos) - 1, dev_h).start()

    for p in range(own_pairs):
        first_amps(p)
    for k in range(len(twos)):
        own_z(1, k)
        own_sibling(1, k)

    found = table_rows(slots, own_pairs, owner_ref, local_ref, fock_ref, (bit_h, bit_y))
    for b in range(QUAD):
        ints, last, weight, keep = found[b]
        to_int, to_float = (ints_in, floats_in) if b == 0 else (ints_out, floats_out)
        to_int[b, 0:slots] = ints
        to_int[b, slots : slots + own_pairs] = last
        to_float[b, 0:slots] = weight
        to_float[b, slots : 2 * slots] = keep

    def push_table(b, which):
        src, dst = ((ints_out, ints_in), (floats_out, floats_in))[which]
        return pltpu.make_async_remote_copy(
            src_ref=src.at[b], dst_ref=dst.at[b], send_sem=table_send.at[which, b], recv_sem=table_recv.at[which, b],
            device_id=((dev_y, dev_y, dev_h, dev_yh)[b],), device_id_type=MESH,
        )

    def load_table(b):
        return pltpu.make_async_copy(ints_in.at[b], table.at[b], table_load.at[b])

    for b in range(1, QUAD):
        push_table(b, 0).start()
        push_table(b, 1).start()
    load_table(0).start()

    def ladder_piece(r, p):
        group = 20 if r == 0 and fitted % 20 == 0 else fitted
        def piece():
            if r == 0:
                loads[p].wait()
            held = amps[r][mine, p]

            def some(g, total):
                for q in range(0, group, 2):
                    one = factors[p, g * group + q]
                    two = factors[p, g * group + q + 1]
                    half = jnp.concatenate(
                        [contract(one, held, 1, 0), contract(two, held, 1, 0)], axis=1
                    ).astype(jnp.bfloat16)
                    total = total + contract(half, jnp.concatenate([one, two], axis=1), 1, 1)
                return total

            total = jnp.zeros((orbitals, orbitals), jnp.float32)
            if group == fitted:
                ladder[p] = some(0, total)
            else:
                ladder[p] = lax.fori_loop(0, fitted // group, some, total)
        return piece

    def margins(b):
        for s in range(slots):
            margin[b, s] = contract(
                rows_basis[b][table[b, s, 0]], group_basis_flat(table[b, s, 1]), 0, 0
            ).astype(jnp.bfloat16)

    def group_basis_flat(q):
        return group_basis[lax.div(q, own_pairs), lax.rem(q, own_pairs)]

    def couple(r, b):
        lefts = []
        for s in range(slots):
            q = table[b, s, 1]
            block = amps[r][lax.div(q, own_pairs), lax.rem(q, own_pairs)]
            lefts.append((contract(margin[b, s], block, 1, 0) * floats_in[b, s : s + 1, :]).astype(jnp.bfloat16))
        total = jnp.zeros((orbitals, orbitals), jnp.float32)
        for s in range(slots):
            keep = floats_in[b, slots + s : slots + s + 1, :] > 0.0
            total = jnp.where(keep, total, 0.0) + contract(lefts[s], margin[b, s], 1, 1)
            sums[b, s] = total

    def partial(b, p):
        return sums[b, table[b, slots + p, 0]]

    def push_y(r, h, k):
        return pltpu.make_async_remote_copy(
            src_ref=to_y.at[r, h, pl.ds(*ends[k])], dst_ref=from_y.at[r, h, pl.ds(*ends[k])],
            send_sem=y_send, recv_sem=y_recv.at[r, h, k],
            device_id=(dev_yh if (h, k) == (0, 0) else dev_y,), device_id_type=MESH,
        )

    def push_z(r, k):
        return pltpu.make_async_remote_copy(
            src_ref=to_z.at[r, pl.ds(*ends[k])], dst_ref=from_z.at[r, pl.ds(*ends[k])],
            send_sem=z_send, recv_sem=z_recv.at[r, k], device_id=(dev_h,), device_id_type=MESH,
        )

    def give_y(r, h, k):
        for p in pairs_of(ends, k):
            to_y[r, h, p] = partial((3, 1)[h], p).astype(jnp.bfloat16)
        push_y(r, h, k).start()

    def give_z(r, k):
        if k > 0:
            push_y(r, 0, k).wait_recv()
        for p in pairs_of(ends, k):
            total = partial(2, p)
            if k > 0:
                total = total + from_y[r, 0, p].astype(jnp.float32)
            to_z[r, p] = total.astype(jnp.bfloat16)
        push_z(r, k).start()

    def update(r, k):
        push_y(r, 1, k).wait_recv()
        push_z(r, k).wait_recv()
        if k == 0:
            push_y(r, 0, k).wait_recv()
        for p in pairs_of(ends, k):
            total = partial(0, p) + from_y[r, 1, p].astype(jnp.float32) + from_z[r, p].astype(jnp.float32) + ladder[p]
            if k == 0:
                total = total + from_y[r, 0, p].astype(jnp.float32)
            esum, divisor, driving = pair_terms(p)
            amplitudes = out_ref[p]
            residual = driving + esum * amplitudes + total
            amplitudes = amplitudes - residual / divisor
            out_ref[p] = amplitudes
            if r + 1 < ITERS:
                amps[r + 1][mine, p] = amplitudes.astype(jnp.bfloat16)
        if r + 1 < ITERS:
            own(r + 2, k)

    for b in range(QUAD):
        sums[b, slots] = jnp.zeros((orbitals, orbitals), jnp.float32)

    def bx(k):
        return came(0, 0, k)

    def bz(k):
        return came(0, 1, k)

    def by(k):
        return row_came(1, k)

    def bh(k):
        return row_came(2, k)

    def fill(p):
        return ladder_piece(0, p)

    def ax(k):
        return came(1, 0, k)

    def az(k):
        return came(1, 1, k)

    def tables_in():
        for b in range(1, QUAD):
            push_table(b, 0).wait_recv()
            push_table(b, 1).wait_recv()
            load_table(b).start()

    number = len(twos)
    fills = [fill(p) for p in range(own_pairs)]
    each = -(-own_pairs // number)
    later = [*range(number // 2, number), *range(number // 2)]
    todo = []
    for k in range(number):
        if k == number - 1:
            todo += [bh(j) for j in range(number // 2)]
        todo += fills[k * each : (k + 1) * each] + [bx(k), bz(k), by(k)]
        if number // 2 - 1 <= k < number - 1:
            first = (k + 1 - number // 2) * 2
            todo += [lambda j=j: own_x(1, j) for j in later[first : first + 2]]
    todo += [tables_in]
    for k in range(number):
        todo += [bh(k)] if k >= number // 2 else []
        todo += [came(0, 2, k)]
    for i in range(number):
        todo += [az(i), ax(later[i])]
        if i == number // 2 - 1:
            todo += [lambda: sibling_done(0)] + [load_table(b).wait for b in range(QUAD)] + [lambda: margins(0)]
    todo += [lambda: margins(1), lambda: margins(2)]
    todo += [row_came(3, k) for k in range(number)] + [lambda: margins(3)]
    todo += [came(1, 2, k) for k in later]
    for event in todo:
        event()
    sibling_done(1)

    number = len(ends)
    early = 2
    for r in range(ITERS):
        rest = [ladder_piece(r, p) for p in range(early, own_pairs)] if r > 0 else []
        more = r + 1 < ITERS

        def ladders(upto):
            while rest and own_pairs - len(rest) < upto:
                rest.pop(0)()

        def both(k):
            if more and k >= 0:
                came(r + 2, 1, k)()
                came(r + 2, 0, k)()

        def diag(k):
            if more and k >= 0:
                came(r + 2, 2, k)()

        couple(r, 3)
        for k in range(4):
            give_y(r, 0, k)
        couple(r, 2)
        give_z(r, 0)
        couple(r, 1)
        give_y(r, 1, 0)
        give_y(r, 0, 4)
        give_y(r, 1, 1)
        give_z(r, 1)
        for k in range(5, number):
            give_y(r, 1, k - 3)
            give_y(r, 0, k)
        for k in range(number - 3, number):
            give_y(r, 1, k)
        couple(r, 0)
        give_z(r, 2)
        ladders(early + 1)
        given = 3
        for k in range(number):
            lo, cnt = ends[k]
            ladders(lo + cnt)
            update(r, k)
            upto = min(number, k + 4 + (k > 0))
            for j in range(given, upto):
                give_z(r, j)
            given = upto
            ladders(early + 2 + k)
            both(k - 2)
            diag(k - 4)
        if more:
            ladder_piece(r + 1, 0)()
            diag(number - 4)
            both(number - 2)
            ladder_piece(r + 1, 1)()
            diag(number - 3)
            diag(number - 2)
            both(number - 1)
            diag(number - 1)
            sibling_done(r + 2)

    for u in range(len(bufs)):
        sends_done(u)
    view = group_basis.at[pl.ds(0, 3)]
    pltpu.make_async_copy(view, view, basis_send).wait()
    for b in range(1, QUAD):
        push_table(b, 0).wait_send()
        push_table(b, 1).wait_send()
    pltpu.make_async_copy(to_y, to_y, y_send).wait()
    pltpu.make_async_copy(to_z, to_z, z_send).wait()


def fused(
    n, pno_basis, pno_count, partner_owner, partner_local, exchange_k, ladder_factor,
    pno_energy, occ_energy, coupling_fock,
):
    own_pairs, domain, orbitals = pno_basis.shape
    partners = partner_owner.shape[1]
    slots = GROUP * (-(-own_pairs * partners // n))
    pieces = max(len(c) for c in cuts(own_pairs))
    smem = pl.BlockSpec(memory_space=pltpu.SMEM)
    vmem = pl.BlockSpec(memory_space=pltpu.VMEM)
    square = (orbitals, orbitals)
    amps = pltpu.VMEM((GROUP, own_pairs) + square, jnp.bfloat16)
    row = pltpu.VMEM((own_pairs, domain, orbitals), jnp.bfloat16)
    ints = pltpu.VMEM((QUAD, slots + own_pairs, 128), jnp.int32)
    floats = pltpu.VMEM((QUAD, 2 * slots, 128), jnp.float32)
    dma = pltpu.SemaphoreType.DMA
    return pl.pallas_call(
        functools.partial(kernel, slots),
        out_shape=jax.ShapeDtypeStruct((own_pairs, orbitals, orbitals), jnp.float32),
        in_specs=[vmem, smem, vmem, vmem, vmem, pl.BlockSpec(memory_space=pl.ANY), vmem, smem, vmem],
        out_specs=vmem,
        scratch_shapes=[
            pltpu.VMEM((GROUP, own_pairs, domain, orbitals), jnp.bfloat16),
            row, row, row, row,
            amps, amps, amps,
            pltpu.VMEM(ladder_factor.shape, jnp.bfloat16),
            pltpu.VMEM((QUAD, slots) + square, jnp.bfloat16),
            pltpu.VMEM((QUAD, slots + 1) + square, jnp.float32),
            pltpu.VMEM((own_pairs,) + square, jnp.float32),
            pltpu.VMEM((ITERS, 2, own_pairs) + square, jnp.bfloat16),
            pltpu.VMEM((ITERS, own_pairs) + square, jnp.bfloat16),
            pltpu.VMEM((ITERS, 2, own_pairs) + square, jnp.bfloat16),
            pltpu.VMEM((ITERS, own_pairs) + square, jnp.bfloat16),
            ints, ints, floats, floats,
            pltpu.SMEM((QUAD, slots + own_pairs, 128), jnp.int32),
            dma((own_pairs,)),
            dma((ITERS + 1, 3, pieces)),
            dma((ITERS + 1,)),
            dma((ITERS + 1,)),
            dma((QUAD, pieces)),
            dma,
            dma((2, QUAD)),
            dma((2, QUAD)),
            dma((QUAD,)),
            dma((ITERS, 2, pieces)),
            dma((ITERS, pieces)),
            dma,
            dma,
        ],
        compiler_params=pltpu.CompilerParams(
            collective_id=0, has_side_effects=True, vmem_limit_bytes=VMEM_BYTES
        ),
        name="jacobi",
    )(
        pno_basis, pno_count, partner_owner, partner_local, exchange_k, ladder_factor,
        pno_energy, occ_energy, coupling_fock,
    )


def shards(*args):
    n = lax.axis_size("pairs")
    own_pairs, domain, orbitals = args[0].shape
    fitted, partners = args[5].shape[1], args[2].shape[1]
    square = orbitals * orbitals
    each = -(-own_pairs * partners // n)
    slots = QUAD * GROUP * each
    held = 2 * own_pairs * orbitals * domain * (GROUP + QUAD + 2) + 2 * args[5].size
    held += square * (2 * ITERS * own_pairs * (GROUP + 6) + slots * 6 + own_pairs * 24)
    fits = held < VMEM_BYTES - (4 << 20)
    exact = n == QUAD * GROUP and own_pairs * partners == n * each
    if exact and own_pairs % 8 == 0 and fitted % 2 == 0 and fits:
        return fused(n, *args)
    return gathered_rows(*args)


def gathered_rows(
    pno_basis,
    pno_count,
    partner_owner,
    partner_local,
    exchange_k,
    ladder_factor,
    pno_energy,
    occ_energy,
    coupling_fock,
):
    own_pairs, domain, orbitals = pno_basis.shape
    fitted = ladder_factor.shape[1]
    partners = partner_owner.shape[1]
    listed = own_pairs * partners
    columns = lax.broadcasted_iota(jnp.int32, (own_pairs, orbitals), 1)
    live_cols = (columns < pno_count[:, None]).astype(jnp.float32)
    masked_basis = pno_basis * live_cols[:, None, :].astype(jnp.bfloat16)
    partner = (partner_owner * own_pairs + partner_local).reshape(listed)

    def rows_of(every):
        return lax.map(lambda i: lax.dynamic_index_in_dim(every, i, 0, keepdims=False), partner)

    every_basis = lax.all_gather(masked_basis, "pairs", axis=0, tiled=True)
    partner_basis = rows_of(every_basis).reshape(own_pairs, partners, domain, orbitals)
    margin = jnp.einsum(
        "rva,rcvb->rcab", masked_basis, partner_basis, preferred_element_type=jnp.float32
    ).astype(jnp.bfloat16)
    energy_sum = pno_energy[:, :, None] + pno_energy[:, None, :] - occ_energy[:, None, None]
    divisor = energy_sum + level_shift
    driving = exchange_k.astype(jnp.float32) * (live_cols[:, :, None] * live_cols[:, None, :])
    amplitudes = -driving / divisor
    weights = coupling_fock.astype(jnp.float32)
    group_width = 8
    for iteration in range(ITERS):
        sent_amps = amplitudes.astype(jnp.bfloat16)
        every_amps = lax.all_gather(sent_amps, "pairs", axis=0, tiled=True)

        def add_group(group_index, total):
            factors = lax.dynamic_slice_in_dim(
                ladder_factor, group_index * group_width, group_width, 1
            )
            ladder_half = jnp.einsum(
                "rqac,rcd->rqad", factors, sent_amps, preferred_element_type=jnp.float32
            ).astype(jnp.bfloat16)
            return total + jnp.einsum(
                "rqad,rqbd->rab", ladder_half, factors, preferred_element_type=jnp.float32
            )

        ladder = lax.fori_loop(
            0,
            fitted // group_width,
            add_group,
            jnp.zeros((own_pairs, orbitals, orbitals), jnp.float32),
        )
        partner_amps = rows_of(every_amps)
        partner_amps = partner_amps.reshape(own_pairs, partners, orbitals, orbitals)
        left_half = jnp.einsum(
            "rcab,rcbd->rcad", margin, partner_amps, preferred_element_type=jnp.float32
        )
        left_half = (left_half * weights[:, :, None, None]).astype(jnp.bfloat16)
        gathered_terms = jnp.einsum(
            "rcad,rced->rcae", left_half, margin, preferred_element_type=jnp.float32
        ).astype(jnp.bfloat16)
        coupled = jnp.sum(gathered_terms, axis=1, dtype=jnp.float32)
        residual = driving + energy_sum * amplitudes + coupled + ladder
        amplitudes = amplitudes - residual / divisor
    return amplitudes


def solution(mesh):
    return jax.shard_map(
        shards,
        mesh=mesh,
        in_specs=(
            P("pairs", None, None),
            P("pairs"),
            P("pairs", None),
            P("pairs", None),
            P("pairs", None, None),
            P("pairs", None, None, None),
            P("pairs", None),
            P("pairs"),
            P("pairs", None),
        ),
        out_specs=P("pairs", None, None),
        check_vma=False,
    )
```

```python
import functools
import jax
import jax.numpy as jnp
from jax import lax
from jax.experimental import pallas as pl
from jax.experimental.pallas import tpu as pltpu
from jax.sharding import PartitionSpec as P

ITERS = 3


level_shift = 0.3
VMEM_BYTES = 67043328
MESH = pl.DeviceIdType.MESH


def contract(a, b, da, db):
    return lax.dot_general(a, b, (((da,), (db,)), ((), ())), preferred_element_type=jnp.float32)


GROUP = 8
QUAD = 4


def cuts(own_pairs):
    twos = tuple((p, 2) for p in range(0, own_pairs, 2))
    inner = tuple((p, 2) for p in range(2, own_pairs // 2, 2))
    ending = tuple((p, 1) for p in range(own_pairs // 2, own_pairs))
    return twos, ((0, 1), (1, 1)) + inner + ending


def table_rows(slots, own_pairs, ref_owner, ref_local, ref_fock, here):
    owner = ref_owner[...]
    local = ref_local[...]
    fock = ref_fock[...].astype(jnp.float32)
    partners = owner.shape[1]
    lane = lax.broadcasted_iota(jnp.int32, owner.shape, 1)
    row = lax.broadcasted_iota(jnp.int32, owner.shape, 0)
    high = lax.shift_right_logical(owner, 4)
    mid = lax.shift_right_logical(owner, 2) & 1
    place = ((lax.shift_right_logical(owner, 3) & 1) * 4 + (owner & 3)) * own_pairs + local
    slot = lax.broadcasted_iota(jnp.int32, (slots, partners), 0)
    slot_wide = lax.broadcasted_iota(jnp.int32, (slots, 128), 0)
    lane_wide = lax.broadcasted_iota(jnp.int32, (slots, 128), 1)
    my_high, my_mid = here
    found = []
    for b in range(QUAD):
        want_high = my_high if b < 2 else 1 - my_high
        want_mid = my_mid if b % 2 == 0 else 1 - my_mid
        chosen = (high == want_high) & (mid == want_mid)
        ones = jnp.where(chosen, 1, 0)
        before = jnp.zeros_like(ones)
        number = jnp.zeros((own_pairs, 1), jnp.int32)
        for c in range(partners):
            before = before + jnp.where(lane > c, ones[:, c : c + 1], 0)
            number = number + ones[:, c : c + 1]
        ahead = jnp.zeros((own_pairs, partners), jnp.int32)
        wide = jnp.broadcast_to(number, (own_pairs, partners))
        for p in range(own_pairs):
            ahead = ahead + jnp.where(row > p, wide[p : p + 1, :], 0)
        rank = jnp.where(chosen, before + ahead, -1)
        pair = jnp.zeros((slots, partners), jnp.int32)
        other = jnp.zeros((slots, partners), jnp.int32)
        weight = jnp.zeros((slots, partners), jnp.float32)
        begins = jnp.zeros((slots, partners), jnp.float32)
        for p in range(own_pairs):
            hit = rank[p : p + 1, :] == slot
            pair = pair + jnp.where(hit, p, 0)
            other = other + jnp.where(hit, place[p : p + 1, :], 0)
            weight = weight + jnp.where(hit, fock[p : p + 1, :], 0.0)
            begins = jnp.where(ahead[p : p + 1, :] == slot, 1.0, begins)
        sums = [jnp.zeros((slots, 1), v.dtype) for v in (pair, other, weight)]
        for c in range(partners):
            sums = [t + v[:, c : c + 1] for t, v in zip(sums, (pair, other, weight))]
        ints = jnp.where(lane_wide == 0, jnp.broadcast_to(sums[0], (slots, 128)), jnp.broadcast_to(sums[1], (slots, 128)))
        last = jnp.where(number > 0, jnp.minimum(ahead[:, 0:1] + number - 1, slots), slots)
        found.append((
            ints,
            jnp.broadcast_to(last, (own_pairs, 128)),
            jnp.broadcast_to(sums[2], (slots, 128)),
            jnp.broadcast_to(1.0 - begins[:, 0:1], (slots, 128)),
        ))
    return found


def kernel(
    slots, basis_ref, count_ref, owner_ref, local_ref, exchange_ref, ladder_hbm, energy_ref,
    occ_ref, fock_ref, out_ref,
    group_basis, row_own, row_y, row_z, row_yz, amps_a, amps_b, amps_c, factors, margin, sums, ladder,
    from_y, from_z, to_y, to_z, ints_out, ints_in, floats_out, floats_in, table,
    load_sem, recv_sem, recv_sib, send_sem, basis_recv, basis_send, table_recv, table_send, table_load,
    y_recv, z_recv, y_send, z_send,
):
    own_pairs, domain, orbitals = basis_ref.shape
    fitted = factors.shape[1]
    me = lax.axis_index("pairs")
    core = me % 2
    bit_x = me // 2 % 2
    bit_y = me // 4 % 2
    bit_l = me // 8 % 2
    bit_h = me // 16
    sibling = me + 1 - 2 * core
    dev_x = me + 2 * (1 - 2 * bit_x)
    dev_y = me + 4 * (1 - 2 * bit_y)
    dev_l = me + 8 * (1 - 2 * bit_l)
    dev_h = me + 16 * (1 - 2 * bit_h)
    dev_d = dev_l + 2 * (1 - 2 * bit_x)
    dev_yh = dev_h + 4 * (1 - 2 * bit_y)
    mine = bit_l * 4 + bit_x * 2 + core
    mine_x = bit_l * 4 + (1 - bit_x) * 2 + core
    mine_l = (1 - bit_l) * 4 + bit_x * 2 + core
    mine_d = (1 - bit_l) * 4 + (1 - bit_x) * 2 + core
    rows_basis = (row_own, row_y, row_z, row_yz)
    bufs = (group_basis, amps_a, amps_b, amps_c)
    amps = (amps_a, amps_b, amps_c)
    twos, ends = cuts(own_pairs)
    cut = (twos, twos, ends, ends)
    ways = [["z"] * len(c) for c in cut]
    for k in range(len(twos) // 2, len(twos)):
        ways[1][k] = "x"
    for u in (2, 3):
        ways[u][-2:] = ["routed", "routed"]

    loads = [
        pltpu.make_async_copy(ladder_hbm.at[p], factors.at[p], load_sem.at[p])
        for p in range(own_pairs)
    ]

    def pairs_of(c, k):
        lo, cnt = c[k]
        return range(lo, lo + cnt)

    def push(u, k, owner, dev, sem):
        view = bufs[u].at[owner, pl.ds(*cut[u][k])]
        return pltpu.make_async_remote_copy(
            src_ref=view, dst_ref=view, send_sem=send_sem.at[u], recv_sem=sem,
            device_id=(dev,), device_id_type=MESH,
        )

    def own_z(u, k):
        push(u, k, mine, dev_l, recv_sem.at[u, 1, k]).start()

    def own_x(u, k):
        push(u, k, mine, dev_x, recv_sem.at[u, 0, k]).start()

    def own(u, k):
        own_z(u, k)
        own_x(u, k)
        if ways[u][k] == "routed":
            push(u, k, mine, dev_d, recv_sem.at[u, 2, k]).start()
        own_sibling(u, k)

    def own_sibling(u, k):
        push(u, k, mine, sibling, recv_sib.at[u]).start()

    def came(u, kind, k):
        def go():
            owner = (mine_x, mine_l, mine_d)[kind]
            push(u, k, owner, sibling, recv_sem.at[u, kind, k]).wait_recv()
            if kind == 0 and ways[u][k] == "x":
                push(u, k, owner, dev_l, recv_sem.at[u, 2, k]).start()
            if kind == 1 and ways[u][k] == "z":
                push(u, k, owner, dev_x, recv_sem.at[u, 2, k]).start()
            push(u, k, owner, sibling, recv_sib.at[u]).start()
        return go

    def sibling_done(u):
        view = bufs[u].at[pl.ds(0, GROUP // 2)]
        pltpu.make_async_copy(view, view, recv_sib.at[u]).wait()

    def sends_done(u):
        view = bufs[u].at[pl.ds(0, GROUP - 1)]
        pltpu.make_async_copy(view, view, send_sem.at[u]).wait()

    def push_row(src, b, k, dev):
        return pltpu.make_async_remote_copy(
            src_ref=src.at[pl.ds(*twos[k])], dst_ref=rows_basis[b].at[pl.ds(*twos[k])],
            send_sem=basis_send, recv_sem=basis_recv.at[b, k],
            device_id=(dev,), device_id_type=MESH,
        )

    def row_came(b, k):
        def go():
            push_row(row_own, b, k, dev_y).wait_recv()
            if b == 2:
                push_row(row_z, 3, k, dev_y).start()
        return go

    lanes = lax.broadcasted_iota(jnp.int32, (orbitals, orbitals), 1)
    rows = lax.broadcasted_iota(jnp.int32, (orbitals, orbitals), 0)
    energy_cols = jnp.transpose(energy_ref[...])

    def pair_terms(p):
        esum = energy_cols[:, p : p + 1] + energy_ref[p : p + 1, :] - occ_ref[p]
        count = count_ref[p]
        live = (lanes < count) & (rows < count)
        driving = jnp.where(live, exchange_ref[p].astype(jnp.float32), 0.0)
        return esum, esum + level_shift, driving

    barrier = pltpu.get_barrier_semaphore()
    near = (sibling, dev_x, dev_l, dev_d, dev_y, dev_h, dev_yh)
    for dev in near:
        pl.semaphore_signal(barrier, inc=1, device_id=(dev,), device_id_type=MESH)
    for load in loads:
        load.start()

    basis_lanes = lax.broadcasted_iota(jnp.int32, (domain, orbitals), 1)

    def mask_basis(p):
        held = jnp.where(
            basis_lanes < count_ref[p], basis_ref[p].astype(jnp.float32), 0.0
        ).astype(jnp.bfloat16)
        group_basis[mine, p] = held
        row_own[p] = held

    def first_amps(p):
        esum, divisor, driving = pair_terms(p)
        first = -driving / divisor
        out_ref[p] = first
        amps_a[mine, p] = first.astype(jnp.bfloat16)

    for p in range(own_pairs):
        mask_basis(p)
    pl.semaphore_wait(barrier, len(near))

    for k in range(len(twos)):
        own(0, k)
        push_row(row_own, 1, k, dev_y).start()
        push_row(row_own, 2, k, dev_h).start()

    for p in range(own_pairs):
        first_amps(p)
    for k in range(len(twos)):
        own_sibling(1, k)

    found = table_rows(slots, own_pairs, owner_ref, local_ref, fock_ref, (bit_h, bit_y))
    for b in range(QUAD):
        ints, last, weight, keep = found[b]
        to_int, to_float = (ints_in, floats_in) if b == 0 else (ints_out, floats_out)
        to_int[b, 0:slots] = ints
        to_int[b, slots : slots + own_pairs] = last
        to_float[b, 0:slots] = weight
        to_float[b, slots : 2 * slots] = keep

    def push_table(b, which):
        src, dst = ((ints_out, ints_in), (floats_out, floats_in))[which]
        return pltpu.make_async_remote_copy(
            src_ref=src.at[b], dst_ref=dst.at[b], send_sem=table_send.at[which, b], recv_sem=table_recv.at[which, b],
            device_id=((dev_y, dev_y, dev_h, dev_yh)[b],), device_id_type=MESH,
        )

    def load_table(b):
        return pltpu.make_async_copy(ints_in.at[b], table.at[b], table_load.at[b])

    for b in range(1, QUAD):
        push_table(b, 0).start()
        push_table(b, 1).start()
    load_table(0).start()

    def ladder_piece(r, p):
        group = 20 if r == 0 and fitted % 20 == 0 else fitted
        def piece():
            if r == 0:
                loads[p].wait()
            held = amps[r][mine, p]

            def some(g, total):
                for q in range(0, group, 2):
                    one = factors[p, g * group + q]
                    two = factors[p, g * group + q + 1]
                    half = jnp.concatenate(
                        [contract(one, held, 1, 0), contract(two, held, 1, 0)], axis=1
                    ).astype(jnp.bfloat16)
                    total = total + contract(half, jnp.concatenate([one, two], axis=1), 1, 1)
                return total

            total = jnp.zeros((orbitals, orbitals), jnp.float32)
            if group == fitted:
                ladder[p] = some(0, total)
            else:
                ladder[p] = lax.fori_loop(0, fitted // group, some, total)
        return piece

    def margins(b):
        for s in range(slots):
            margin[b, s] = contract(
                rows_basis[b][table[b, s, 0]], group_basis_flat(table[b, s, 1]), 0, 0
            ).astype(jnp.bfloat16)

    def group_basis_flat(q):
        return group_basis[lax.div(q, own_pairs), lax.rem(q, own_pairs)]

    def couple(r, b):
        lefts = []
        for s in range(slots):
            q = table[b, s, 1]
            block = amps[r][lax.div(q, own_pairs), lax.rem(q, own_pairs)]
            lefts.append((contract(margin[b, s], block, 1, 0) * floats_in[b, s : s + 1, :]).astype(jnp.bfloat16))
        total = jnp.zeros((orbitals, orbitals), jnp.float32)
        for s in range(slots):
            keep = floats_in[b, slots + s : slots + s + 1, :] > 0.0
            total = jnp.where(keep, total, 0.0) + contract(lefts[s], margin[b, s], 1, 1)
            sums[b, s] = total

    def partial(b, p):
        return sums[b, table[b, slots + p, 0]]

    def push_y(r, h, k):
        return pltpu.make_async_remote_copy(
            src_ref=to_y.at[r, h, pl.ds(*ends[k])], dst_ref=from_y.at[r, h, pl.ds(*ends[k])],
            send_sem=y_send, recv_sem=y_recv.at[r, h, k],
            device_id=(dev_yh if (h, k) == (0, 0) else dev_y,), device_id_type=MESH,
        )

    def push_z(r, k):
        return pltpu.make_async_remote_copy(
            src_ref=to_z.at[r, pl.ds(*ends[k])], dst_ref=from_z.at[r, pl.ds(*ends[k])],
            send_sem=z_send, recv_sem=z_recv.at[r, k], device_id=(dev_h,), device_id_type=MESH,
        )

    def give_y(r, h, k):
        for p in pairs_of(ends, k):
            to_y[r, h, p] = partial((3, 1)[h], p).astype(jnp.bfloat16)
        push_y(r, h, k).start()

    def give_z(r, k):
        if k > 0:
            push_y(r, 0, k).wait_recv()
        for p in pairs_of(ends, k):
            total = partial(2, p)
            if k > 0:
                total = total + from_y[r, 0, p].astype(jnp.float32)
            to_z[r, p] = total.astype(jnp.bfloat16)
        push_z(r, k).start()

    def update(r, k):
        push_y(r, 1, k).wait_recv()
        push_z(r, k).wait_recv()
        if k == 0:
            push_y(r, 0, k).wait_recv()
        for p in pairs_of(ends, k):
            total = partial(0, p) + from_y[r, 1, p].astype(jnp.float32) + from_z[r, p].astype(jnp.float32) + ladder[p]
            if k == 0:
                total = total + from_y[r, 0, p].astype(jnp.float32)
            esum, divisor, driving = pair_terms(p)
            amplitudes = out_ref[p]
            residual = driving + esum * amplitudes + total
            amplitudes = amplitudes - residual / divisor
            out_ref[p] = amplitudes
            if r + 1 < ITERS:
                amps[r + 1][mine, p] = amplitudes.astype(jnp.bfloat16)
        if r + 1 < ITERS:
            own(r + 2, k)

    for b in range(QUAD):
        sums[b, slots] = jnp.zeros((orbitals, orbitals), jnp.float32)

    def bx(k):
        return came(0, 0, k)

    def bz(k):
        return came(0, 1, k)

    def by(k):
        return row_came(1, k)

    def bh(k):
        return row_came(2, k)

    def fill(p):
        return ladder_piece(0, p)

    def ax(k):
        return came(1, 0, k)

    def az(k):
        return came(1, 1, k)

    def tables_in():
        for b in range(1, QUAD):
            push_table(b, 0).wait_recv()
            push_table(b, 1).wait_recv()
            load_table(b).start()

    number = len(twos)
    fills = [fill(p) for p in range(own_pairs)]
    each = -(-own_pairs // number)
    later = [*range(number // 2, number), *range(number // 2)]
    todo = []
    for k in range(number):
        if k == number - 1:
            todo += [bh(j) for j in range(number // 2)]
        todo += fills[k * each : (k + 1) * each] + [bx(k), bz(k), by(k)]
        if number // 2 - 1 <= k < number - 1:
            first = (k + 1 - number // 2) * 2
            todo += [lambda j=j: own_x(1, j) for j in later[first : first + 2]]
            todo += [lambda j=j: own_z(1, j) for j in range(first, first + 2)]
    todo += [tables_in]
    for k in range(number):
        todo += [bh(k)] if k >= number // 2 else []
        todo += [came(0, 2, k)]
    for i in range(number):
        todo += [az(i), ax(later[i])]
        if i == number // 2 - 1:
            todo += [lambda: sibling_done(0)] + [load_table(b).wait for b in range(QUAD)] + [lambda: margins(0)]
    todo += [lambda: margins(1), lambda: margins(2)]
    todo += [row_came(3, k) for k in range(number)] + [lambda: margins(3)]
    todo += [came(1, 2, k) for k in later]
    for event in todo:
        event()
    sibling_done(1)

    number = len(ends)
    early = 2
    for r in range(ITERS):
        rest = [ladder_piece(r, p) for p in range(early, own_pairs)] if r > 0 else []
        more = r + 1 < ITERS

        def ladders(upto):
            while rest and own_pairs - len(rest) < upto:
                rest.pop(0)()

        def both(k):
            if more and k >= 0:
                came(r + 2, 1, k)()
                came(r + 2, 0, k)()

        def diag(k):
            if more and k >= 0:
                came(r + 2, 2, k)()

        couple(r, 3)
        for k in range(4):
            give_y(r, 0, k)
        couple(r, 2)
        give_z(r, 0)
        couple(r, 1)
        give_y(r, 1, 0)
        give_y(r, 0, 4)
        give_y(r, 1, 1)
        give_z(r, 1)
        for k in range(5, number):
            give_y(r, 1, k - 3)
            give_y(r, 0, k)
        for k in range(number - 3, number):
            give_y(r, 1, k)
        couple(r, 0)
        give_z(r, 2)
        ladders(early + 1)
        given = 3
        for k in range(number):
            lo, cnt = ends[k]
            ladders(lo + cnt)
            update(r, k)
            upto = min(number, k + 4 + (k > 0))
            for j in range(given, upto):
                give_z(r, j)
            given = upto
            ladders(early + 2 + k)
            both(k - 2)
            diag(k - 4)
        if more:
            ladder_piece(r + 1, 0)()
            diag(number - 4)
            both(number - 2)
            ladder_piece(r + 1, 1)()
            diag(number - 3)
            diag(number - 2)
            both(number - 1)
            diag(number - 1)
            sibling_done(r + 2)

    for u in range(len(bufs)):
        sends_done(u)
    view = group_basis.at[pl.ds(0, 3)]
    pltpu.make_async_copy(view, view, basis_send).wait()
    for b in range(1, QUAD):
        push_table(b, 0).wait_send()
        push_table(b, 1).wait_send()
    pltpu.make_async_copy(to_y, to_y, y_send).wait()
    pltpu.make_async_copy(to_z, to_z, z_send).wait()


def fused(
    n, pno_basis, pno_count, partner_owner, partner_local, exchange_k, ladder_factor,
    pno_energy, occ_energy, coupling_fock,
):
    own_pairs, domain, orbitals = pno_basis.shape
    partners = partner_owner.shape[1]
    slots = GROUP * (-(-own_pairs * partners // n))
    pieces = max(len(c) for c in cuts(own_pairs))
    smem = pl.BlockSpec(memory_space=pltpu.SMEM)
    vmem = pl.BlockSpec(memory_space=pltpu.VMEM)
    square = (orbitals, orbitals)
    amps = pltpu.VMEM((GROUP, own_pairs) + square, jnp.bfloat16)
    row = pltpu.VMEM((own_pairs, domain, orbitals), jnp.bfloat16)
    ints = pltpu.VMEM((QUAD, slots + own_pairs, 128), jnp.int32)
    floats = pltpu.VMEM((QUAD, 2 * slots, 128), jnp.float32)
    dma = pltpu.SemaphoreType.DMA
    return pl.pallas_call(
        functools.partial(kernel, slots),
        out_shape=jax.ShapeDtypeStruct((own_pairs, orbitals, orbitals), jnp.float32),
        in_specs=[vmem, smem, vmem, vmem, vmem, pl.BlockSpec(memory_space=pl.ANY), vmem, smem, vmem],
        out_specs=vmem,
        scratch_shapes=[
            pltpu.VMEM((GROUP, own_pairs, domain, orbitals), jnp.bfloat16),
            row, row, row, row,
            amps, amps, amps,
            pltpu.VMEM(ladder_factor.shape, jnp.bfloat16),
            pltpu.VMEM((QUAD, slots) + square, jnp.bfloat16),
            pltpu.VMEM((QUAD, slots + 1) + square, jnp.float32),
            pltpu.VMEM((own_pairs,) + square, jnp.float32),
            pltpu.VMEM((ITERS, 2, own_pairs) + square, jnp.bfloat16),
            pltpu.VMEM((ITERS, own_pairs) + square, jnp.bfloat16),
            pltpu.VMEM((ITERS, 2, own_pairs) + square, jnp.bfloat16),
            pltpu.VMEM((ITERS, own_pairs) + square, jnp.bfloat16),
            ints, ints, floats, floats,
            pltpu.SMEM((QUAD, slots + own_pairs, 128), jnp.int32),
            dma((own_pairs,)),
            dma((ITERS + 1, 3, pieces)),
            dma((ITERS + 1,)),
            dma((ITERS + 1,)),
            dma((QUAD, pieces)),
            dma,
            dma((2, QUAD)),
            dma((2, QUAD)),
            dma((QUAD,)),
            dma((ITERS, 2, pieces)),
            dma((ITERS, pieces)),
            dma,
            dma,
        ],
        compiler_params=pltpu.CompilerParams(
            collective_id=0, has_side_effects=True, vmem_limit_bytes=VMEM_BYTES
        ),
        name="jacobi",
    )(
        pno_basis, pno_count, partner_owner, partner_local, exchange_k, ladder_factor,
        pno_energy, occ_energy, coupling_fock,
    )


def shards(*args):
    n = lax.axis_size("pairs")
    own_pairs, domain, orbitals = args[0].shape
    fitted, partners = args[5].shape[1], args[2].shape[1]
    square = orbitals * orbitals
    each = -(-own_pairs * partners // n)
    slots = QUAD * GROUP * each
    held = 2 * own_pairs * orbitals * domain * (GROUP + QUAD + 2) + 2 * args[5].size
    held += square * (2 * ITERS * own_pairs * (GROUP + 6) + slots * 6 + own_pairs * 24)
    fits = held < VMEM_BYTES - (4 << 20)
    exact = n == QUAD * GROUP and own_pairs * partners == n * each
    if exact and own_pairs % 8 == 0 and fitted % 2 == 0 and fits:
        return fused(n, *args)
    return gathered_rows(*args)


def gathered_rows(
    pno_basis,
    pno_count,
    partner_owner,
    partner_local,
    exchange_k,
    ladder_factor,
    pno_energy,
    occ_energy,
    coupling_fock,
):
    own_pairs, domain, orbitals = pno_basis.shape
    fitted = ladder_factor.shape[1]
    partners = partner_owner.shape[1]
    listed = own_pairs * partners
    columns = lax.broadcasted_iota(jnp.int32, (own_pairs, orbitals), 1)
    live_cols = (columns < pno_count[:, None]).astype(jnp.float32)
    masked_basis = pno_basis * live_cols[:, None, :].astype(jnp.bfloat16)
    partner = (partner_owner * own_pairs + partner_local).reshape(listed)

    def rows_of(every):
        return lax.map(lambda i: lax.dynamic_index_in_dim(every, i, 0, keepdims=False), partner)

    every_basis = lax.all_gather(masked_basis, "pairs", axis=0, tiled=True)
    partner_basis = rows_of(every_basis).reshape(own_pairs, partners, domain, orbitals)
    margin = jnp.einsum(
        "rva,rcvb->rcab", masked_basis, partner_basis, preferred_element_type=jnp.float32
    ).astype(jnp.bfloat16)
    energy_sum = pno_energy[:, :, None] + pno_energy[:, None, :] - occ_energy[:, None, None]
    divisor = energy_sum + level_shift
    driving = exchange_k.astype(jnp.float32) * (live_cols[:, :, None] * live_cols[:, None, :])
    amplitudes = -driving / divisor
    weights = coupling_fock.astype(jnp.float32)
    group_width = 8
    for iteration in range(ITERS):
        sent_amps = amplitudes.astype(jnp.bfloat16)
        every_amps = lax.all_gather(sent_amps, "pairs", axis=0, tiled=True)

        def add_group(group_index, total):
            factors = lax.dynamic_slice_in_dim(
                ladder_factor, group_index * group_width, group_width, 1
            )
            ladder_half = jnp.einsum(
                "rqac,rcd->rqad", factors, sent_amps, preferred_element_type=jnp.float32
            ).astype(jnp.bfloat16)
            return total + jnp.einsum(
                "rqad,rqbd->rab", ladder_half, factors, preferred_element_type=jnp.float32
            )

        ladder = lax.fori_loop(
            0,
            fitted // group_width,
            add_group,
            jnp.zeros((own_pairs, orbitals, orbitals), jnp.float32),
        )
        partner_amps = rows_of(every_amps)
        partner_amps = partner_amps.reshape(own_pairs, partners, orbitals, orbitals)
        left_half = jnp.einsum(
            "rcab,rcbd->rcad", margin, partner_amps, preferred_element_type=jnp.float32
        )
        left_half = (left_half * weights[:, :, None, None]).astype(jnp.bfloat16)
        gathered_terms = jnp.einsum(
            "rcad,rced->rcae", left_half, margin, preferred_element_type=jnp.float32
        ).astype(jnp.bfloat16)
        coupled = jnp.sum(gathered_terms, axis=1, dtype=jnp.float32)
        residual = driving + energy_sum * amplitudes + coupled + ladder
        amplitudes = amplitudes - residual / divisor
    return amplitudes


def solution(mesh):
    return jax.shard_map(
        shards,
        mesh=mesh,
        in_specs=(
            P("pairs", None, None),
            P("pairs"),
            P("pairs", None),
            P("pairs", None),
            P("pairs", None, None),
            P("pairs", None, None, None),
            P("pairs", None),
            P("pairs"),
            P("pairs", None),
        ),
        out_specs=P("pairs", None, None),
        check_vma=False,
    )
```

```python
import functools
import jax
import jax.numpy as jnp
from jax import lax
from jax.experimental import pallas as pl
from jax.experimental.pallas import tpu as pltpu
from jax.sharding import PartitionSpec as P

ITERS = 3


level_shift = 0.3
VMEM_BYTES = 67043328
MESH = pl.DeviceIdType.MESH


def contract(a, b, da, db):
    return lax.dot_general(a, b, (((da,), (db,)), ((), ())), preferred_element_type=jnp.float32)


GROUP = 8
QUAD = 4


def cuts(own_pairs):
    twos = tuple((p, 2) for p in range(0, own_pairs, 2))
    inner = tuple((p, 2) for p in range(2, own_pairs // 2, 2))
    ending = tuple((p, 1) for p in range(own_pairs // 2, own_pairs))
    return twos, ((0, 1), (1, 1)) + inner + ending


def table_rows(slots, own_pairs, ref_owner, ref_local, ref_fock, here):
    owner = ref_owner[...]
    local = ref_local[...]
    fock = ref_fock[...].astype(jnp.float32)
    partners = owner.shape[1]
    lane = lax.broadcasted_iota(jnp.int32, owner.shape, 1)
    row = lax.broadcasted_iota(jnp.int32, owner.shape, 0)
    high = lax.shift_right_logical(owner, 4)
    mid = lax.shift_right_logical(owner, 2) & 1
    place = ((lax.shift_right_logical(owner, 3) & 1) * 4 + (owner & 3)) * own_pairs + local
    slot = lax.broadcasted_iota(jnp.int32, (slots, partners), 0)
    slot_wide = lax.broadcasted_iota(jnp.int32, (slots, 128), 0)
    lane_wide = lax.broadcasted_iota(jnp.int32, (slots, 128), 1)
    my_high, my_mid = here
    found = []
    for b in range(QUAD):
        want_high = my_high if b < 2 else 1 - my_high
        want_mid = my_mid if b % 2 == 0 else 1 - my_mid
        chosen = (high == want_high) & (mid == want_mid)
        ones = jnp.where(chosen, 1, 0)
        before = jnp.zeros_like(ones)
        number = jnp.zeros((own_pairs, 1), jnp.int32)
        for c in range(partners):
            before = before + jnp.where(lane > c, ones[:, c : c + 1], 0)
            number = number + ones[:, c : c + 1]
        ahead = jnp.zeros((own_pairs, partners), jnp.int32)
        wide = jnp.broadcast_to(number, (own_pairs, partners))
        for p in range(own_pairs):
            ahead = ahead + jnp.where(row > p, wide[p : p + 1, :], 0)
        rank = jnp.where(chosen, before + ahead, -1)
        pair = jnp.zeros((slots, partners), jnp.int32)
        other = jnp.zeros((slots, partners), jnp.int32)
        weight = jnp.zeros((slots, partners), jnp.float32)
        begins = jnp.zeros((slots, partners), jnp.float32)
        for p in range(own_pairs):
            hit = rank[p : p + 1, :] == slot
            pair = pair + jnp.where(hit, p, 0)
            other = other + jnp.where(hit, place[p : p + 1, :], 0)
            weight = weight + jnp.where(hit, fock[p : p + 1, :], 0.0)
            begins = jnp.where(ahead[p : p + 1, :] == slot, 1.0, begins)
        sums = [jnp.zeros((slots, 1), v.dtype) for v in (pair, other, weight)]
        for c in range(partners):
            sums = [t + v[:, c : c + 1] for t, v in zip(sums, (pair, other, weight))]
        ints = jnp.where(lane_wide == 0, jnp.broadcast_to(sums[0], (slots, 128)), jnp.broadcast_to(sums[1], (slots, 128)))
        last = jnp.where(number > 0, jnp.minimum(ahead[:, 0:1] + number - 1, slots), slots)
        found.append((
            ints,
            jnp.broadcast_to(last, (own_pairs, 128)),
            jnp.broadcast_to(sums[2], (slots, 128)),
            jnp.broadcast_to(1.0 - begins[:, 0:1], (slots, 128)),
        ))
    return found


def kernel(
    slots, basis_ref, count_ref, owner_ref, local_ref, exchange_ref, ladder_hbm, energy_ref,
    occ_ref, fock_ref, result_hbm,
    group_basis, row_own, row_y, row_z, row_yz, amps_a, amps_b, amps_c, factors, margin, sums, ladder,
    from_y, from_z, to_y, to_z, ints_out, ints_in, floats_out, floats_in, table,
    load_sem, recv_sem, recv_sib, send_sem, basis_recv, basis_send, table_recv, table_send, table_load,
    y_recv, z_recv, y_send, z_send, out_ref, result_sem,
):
    own_pairs, domain, orbitals = basis_ref.shape
    fitted = factors.shape[1]
    me = lax.axis_index("pairs")
    core = me % 2
    bit_x = me // 2 % 2
    bit_y = me // 4 % 2
    bit_l = me // 8 % 2
    bit_h = me // 16
    sibling = me + 1 - 2 * core
    dev_x = me + 2 * (1 - 2 * bit_x)
    dev_y = me + 4 * (1 - 2 * bit_y)
    dev_l = me + 8 * (1 - 2 * bit_l)
    dev_h = me + 16 * (1 - 2 * bit_h)
    dev_d = dev_l + 2 * (1 - 2 * bit_x)
    dev_yh = dev_h + 4 * (1 - 2 * bit_y)
    mine = bit_l * 4 + bit_x * 2 + core
    mine_x = bit_l * 4 + (1 - bit_x) * 2 + core
    mine_l = (1 - bit_l) * 4 + bit_x * 2 + core
    mine_d = (1 - bit_l) * 4 + (1 - bit_x) * 2 + core
    rows_basis = (row_own, row_y, row_z, row_yz)
    bufs = (group_basis, amps_a, amps_b, amps_c)
    amps = (amps_a, amps_b, amps_c)
    twos, ends = cuts(own_pairs)
    cut = (twos, twos, ends, ends)
    ways = [["z"] * len(c) for c in cut]
    for k in range(len(twos) // 2, len(twos)):
        ways[1][k] = "x"
    for u in (2, 3):
        ways[u][-2:] = ["routed", "routed"]

    loads = [
        pltpu.make_async_copy(ladder_hbm.at[p], factors.at[p], load_sem.at[p])
        for p in range(own_pairs)
    ]

    def pairs_of(c, k):
        lo, cnt = c[k]
        return range(lo, lo + cnt)

    def push(u, k, owner, dev, sem):
        view = bufs[u].at[owner, pl.ds(*cut[u][k])]
        return pltpu.make_async_remote_copy(
            src_ref=view, dst_ref=view, send_sem=send_sem.at[u], recv_sem=sem,
            device_id=(dev,), device_id_type=MESH,
        )

    def own_z(u, k):
        push(u, k, mine, dev_l, recv_sem.at[u, 1, k]).start()

    def own_x(u, k):
        push(u, k, mine, dev_x, recv_sem.at[u, 0, k]).start()

    def own(u, k):
        own_z(u, k)
        own_x(u, k)
        if ways[u][k] == "routed":
            push(u, k, mine, dev_d, recv_sem.at[u, 2, k]).start()
        own_sibling(u, k)

    def own_sibling(u, k):
        push(u, k, mine, sibling, recv_sib.at[u]).start()

    def came(u, kind, k):
        def go():
            owner = (mine_x, mine_l, mine_d)[kind]
            push(u, k, owner, sibling, recv_sem.at[u, kind, k]).wait_recv()
            if kind == 0 and ways[u][k] == "x":
                push(u, k, owner, dev_l, recv_sem.at[u, 2, k]).start()
            if kind == 1 and ways[u][k] == "z":
                push(u, k, owner, dev_x, recv_sem.at[u, 2, k]).start()
            push(u, k, owner, sibling, recv_sib.at[u]).start()
        return go

    def sibling_done(u):
        view = bufs[u].at[pl.ds(0, GROUP // 2)]
        pltpu.make_async_copy(view, view, recv_sib.at[u]).wait()

    def sends_done(u):
        view = bufs[u].at[pl.ds(0, GROUP - 1)]
        pltpu.make_async_copy(view, view, send_sem.at[u]).wait()

    def push_row(src, b, k, dev):
        return pltpu.make_async_remote_copy(
            src_ref=src.at[pl.ds(*twos[k])], dst_ref=rows_basis[b].at[pl.ds(*twos[k])],
            send_sem=basis_send, recv_sem=basis_recv.at[b, k],
            device_id=(dev,), device_id_type=MESH,
        )

    def row_came(b, k):
        def go():
            push_row(row_own, b, k, dev_y).wait_recv()
            if b == 2:
                push_row(row_z, 3, k, dev_y).start()
        return go

    lanes = lax.broadcasted_iota(jnp.int32, (orbitals, orbitals), 1)
    rows = lax.broadcasted_iota(jnp.int32, (orbitals, orbitals), 0)
    energy_cols = jnp.transpose(energy_ref[...])

    def pair_terms(p):
        esum = energy_cols[:, p : p + 1] + energy_ref[p : p + 1, :] - occ_ref[p]
        count = count_ref[p]
        live = (lanes < count) & (rows < count)
        driving = jnp.where(live, exchange_ref[p].astype(jnp.float32), 0.0)
        return esum, esum + level_shift, driving

    barrier = pltpu.get_barrier_semaphore()
    near = (sibling, dev_x, dev_l, dev_d, dev_y, dev_h, dev_yh)
    for dev in near:
        pl.semaphore_signal(barrier, inc=1, device_id=(dev,), device_id_type=MESH)
    for load in loads:
        load.start()

    basis_lanes = lax.broadcasted_iota(jnp.int32, (domain, orbitals), 1)

    def mask_basis(p):
        held = jnp.where(
            basis_lanes < count_ref[p], basis_ref[p].astype(jnp.float32), 0.0
        ).astype(jnp.bfloat16)
        group_basis[mine, p] = held
        row_own[p] = held

    def first_amps(p):
        esum, divisor, driving = pair_terms(p)
        first = -driving / divisor
        out_ref[p] = first
        amps_a[mine, p] = first.astype(jnp.bfloat16)

    for p in range(own_pairs):
        mask_basis(p)
    pl.semaphore_wait(barrier, len(near))

    for k in range(len(twos)):
        own(0, k)
        push_row(row_own, 1, k, dev_y).start()
        push_row(row_own, 2, k, dev_h).start()

    for p in range(own_pairs):
        first_amps(p)
    for k in range(len(twos)):
        own_sibling(1, k)

    found = table_rows(slots, own_pairs, owner_ref, local_ref, fock_ref, (bit_h, bit_y))
    for b in range(QUAD):
        ints, last, weight, keep = found[b]
        to_int, to_float = (ints_in, floats_in) if b == 0 else (ints_out, floats_out)
        to_int[b, 0:slots] = ints
        to_int[b, slots : slots + own_pairs] = last
        to_float[b, 0:slots] = weight
        to_float[b, slots : 2 * slots] = keep

    def push_table(b, which):
        src, dst = ((ints_out, ints_in), (floats_out, floats_in))[which]
        return pltpu.make_async_remote_copy(
            src_ref=src.at[b], dst_ref=dst.at[b], send_sem=table_send.at[which, b], recv_sem=table_recv.at[which, b],
            device_id=((dev_y, dev_y, dev_h, dev_yh)[b],), device_id_type=MESH,
        )

    def load_table(b):
        return pltpu.make_async_copy(ints_in.at[b], table.at[b], table_load.at[b])

    for b in range(1, QUAD):
        push_table(b, 0).start()
        push_table(b, 1).start()
    load_table(0).start()

    def ladder_piece(r, p):
        group = 20 if r == 0 and fitted % 20 == 0 else fitted
        def piece():
            if r == 0:
                loads[p].wait()
            held = amps[r][mine, p]

            def some(g, total):
                for q in range(0, group, 2):
                    one = factors[p, g * group + q]
                    two = factors[p, g * group + q + 1]
                    half = jnp.concatenate(
                        [contract(one, held, 1, 0), contract(two, held, 1, 0)], axis=1
                    ).astype(jnp.bfloat16)
                    total = total + contract(half, jnp.concatenate([one, two], axis=1), 1, 1)
                return total

            total = jnp.zeros((orbitals, orbitals), jnp.float32)
            if group == fitted:
                ladder[p] = some(0, total)
            else:
                ladder[p] = lax.fori_loop(0, fitted // group, some, total)
        return piece

    def margins(b):
        for s in range(slots):
            margin[b, s] = contract(
                rows_basis[b][table[b, s, 0]], group_basis_flat(table[b, s, 1]), 0, 0
            ).astype(jnp.bfloat16)

    def group_basis_flat(q):
        return group_basis[lax.div(q, own_pairs), lax.rem(q, own_pairs)]

    def couple(r, b):
        lefts = []
        for s in range(slots):
            q = table[b, s, 1]
            block = amps[r][lax.div(q, own_pairs), lax.rem(q, own_pairs)]
            lefts.append((contract(margin[b, s], block, 1, 0) * floats_in[b, s : s + 1, :]).astype(jnp.bfloat16))
        total = jnp.zeros((orbitals, orbitals), jnp.float32)
        for s in range(slots):
            keep = floats_in[b, slots + s : slots + s + 1, :] > 0.0
            total = jnp.where(keep, total, 0.0) + contract(lefts[s], margin[b, s], 1, 1)
            sums[b, s] = total

    def partial(b, p):
        return sums[b, table[b, slots + p, 0]]

    def push_y(r, h, k):
        return pltpu.make_async_remote_copy(
            src_ref=to_y.at[r, h, pl.ds(*ends[k])], dst_ref=from_y.at[r, h, pl.ds(*ends[k])],
            send_sem=y_send, recv_sem=y_recv.at[r, h, k],
            device_id=(dev_yh if (h, k) == (0, 0) else dev_y,), device_id_type=MESH,
        )

    def push_z(r, k):
        return pltpu.make_async_remote_copy(
            src_ref=to_z.at[r, pl.ds(*ends[k])], dst_ref=from_z.at[r, pl.ds(*ends[k])],
            send_sem=z_send, recv_sem=z_recv.at[r, k], device_id=(dev_h,), device_id_type=MESH,
        )

    def give_y(r, h, k):
        for p in pairs_of(ends, k):
            to_y[r, h, p] = partial((3, 1)[h], p).astype(jnp.bfloat16)
        push_y(r, h, k).start()

    def give_z(r, k):
        if k > 0:
            push_y(r, 0, k).wait_recv()
        for p in pairs_of(ends, k):
            total = partial(2, p)
            if k > 0:
                total = total + from_y[r, 0, p].astype(jnp.float32)
            to_z[r, p] = total.astype(jnp.bfloat16)
        push_z(r, k).start()

    def update(r, k):
        push_y(r, 1, k).wait_recv()
        push_z(r, k).wait_recv()
        if k == 0:
            push_y(r, 0, k).wait_recv()
        for p in pairs_of(ends, k):
            total = partial(0, p) + from_y[r, 1, p].astype(jnp.float32) + from_z[r, p].astype(jnp.float32) + ladder[p]
            if k == 0:
                total = total + from_y[r, 0, p].astype(jnp.float32)
            esum, divisor, driving = pair_terms(p)
            amplitudes = out_ref[p]
            residual = driving + esum * amplitudes + total
            amplitudes = amplitudes - residual / divisor
            out_ref[p] = amplitudes
            if r + 1 < ITERS:
                amps[r + 1][mine, p] = amplitudes.astype(jnp.bfloat16)
        if r + 1 < ITERS:
            own(r + 2, k)
        else:
            place = pl.ds(*ends[k])
            pltpu.make_async_copy(out_ref.at[place], result_hbm.at[place], result_sem).start()

    for b in range(QUAD):
        sums[b, slots] = jnp.zeros((orbitals, orbitals), jnp.float32)

    def bx(k):
        return came(0, 0, k)

    def bz(k):
        return came(0, 1, k)

    def by(k):
        return row_came(1, k)

    def bh(k):
        return row_came(2, k)

    def fill(p):
        return ladder_piece(0, p)

    def ax(k):
        return came(1, 0, k)

    def az(k):
        return came(1, 1, k)

    def tables_in():
        for b in range(1, QUAD):
            push_table(b, 0).wait_recv()
            push_table(b, 1).wait_recv()
            load_table(b).start()

    number = len(twos)
    fills = [fill(p) for p in range(own_pairs)]
    each = -(-own_pairs // number)
    later = [*range(number // 2, number), *range(number // 2)]
    todo = []
    for k in range(number):
        if k == number - 1:
            todo += [bh(j) for j in range(number // 2)]
        todo += fills[k * each : (k + 1) * each] + [bx(k), bz(k), by(k)]
        if number // 2 - 1 <= k < number - 1:
            first = (k + 1 - number // 2) * 2
            todo += [lambda j=j: own_x(1, j) for j in later[first : first + 2]]
            todo += [lambda j=j: own_z(1, j) for j in range(first, first + 2)]
    todo += [tables_in]
    for k in range(number):
        todo += [bh(k)] if k >= number // 2 else []
        todo += [came(0, 2, k)]
    for i in range(number):
        todo += [az(i), ax(later[i])]
        if i == number // 2 - 1:
            todo += [lambda: sibling_done(0)] + [load_table(b).wait for b in range(QUAD)] + [lambda: margins(0)]
    todo += [lambda: margins(1), lambda: margins(2)]
    todo += [row_came(3, k) for k in range(number)] + [lambda: margins(3)]
    todo += [came(1, 2, k) for k in later]
    for event in todo:
        event()
    sibling_done(1)

    number = len(ends)
    early = 2
    for r in range(ITERS):
        rest = [ladder_piece(r, p) for p in range(early, own_pairs)] if r > 0 else []
        more = r + 1 < ITERS

        def ladders(upto):
            while rest and own_pairs - len(rest) < upto:
                rest.pop(0)()

        def both(k):
            if more and k >= 0:
                came(r + 2, 1, k)()
                came(r + 2, 0, k)()

        def diag(k):
            if more and k >= 0:
                came(r + 2, 2, k)()

        couple(r, 3)
        for k in range(4):
            give_y(r, 0, k)
        couple(r, 2)
        give_z(r, 0)
        couple(r, 1)
        give_y(r, 1, 0)
        give_y(r, 0, 4)
        give_y(r, 1, 1)
        give_z(r, 1)
        for k in range(5, number):
            give_y(r, 1, k - 3)
            give_y(r, 0, k)
        for k in range(number - 3, number):
            give_y(r, 1, k)
        couple(r, 0)
        give_z(r, 2)
        ladders(early + 1)
        given = 3
        for k in range(number):
            lo, cnt = ends[k]
            ladders(lo + cnt)
            update(r, k)
            upto = min(number, k + 4 + (k > 0))
            for j in range(given, upto):
                give_z(r, j)
            given = upto
            ladders(early + 2 + k)
            both(k - 2)
            diag(k - 4)
        if more:
            ladder_piece(r + 1, 0)()
            diag(number - 4)
            both(number - 2)
            ladder_piece(r + 1, 1)()
            diag(number - 3)
            diag(number - 2)
            both(number - 1)
            diag(number - 1)
            sibling_done(r + 2)

    for u in range(len(bufs)):
        sends_done(u)
    view = group_basis.at[pl.ds(0, 3)]
    pltpu.make_async_copy(view, view, basis_send).wait()
    for b in range(1, QUAD):
        push_table(b, 0).wait_send()
        push_table(b, 1).wait_send()
    pltpu.make_async_copy(to_y, to_y, y_send).wait()
    pltpu.make_async_copy(to_z, to_z, z_send).wait()
    pltpu.make_async_copy(out_ref, result_hbm, result_sem).wait()


def fused(
    n, pno_basis, pno_count, partner_owner, partner_local, exchange_k, ladder_factor,
    pno_energy, occ_energy, coupling_fock,
):
    own_pairs, domain, orbitals = pno_basis.shape
    partners = partner_owner.shape[1]
    slots = GROUP * (-(-own_pairs * partners // n))
    pieces = max(len(c) for c in cuts(own_pairs))
    smem = pl.BlockSpec(memory_space=pltpu.SMEM)
    vmem = pl.BlockSpec(memory_space=pltpu.VMEM)
    square = (orbitals, orbitals)
    amps = pltpu.VMEM((GROUP, own_pairs) + square, jnp.bfloat16)
    row = pltpu.VMEM((own_pairs, domain, orbitals), jnp.bfloat16)
    ints = pltpu.VMEM((QUAD, slots + own_pairs, 128), jnp.int32)
    floats = pltpu.VMEM((QUAD, 2 * slots, 128), jnp.float32)
    dma = pltpu.SemaphoreType.DMA
    return pl.pallas_call(
        functools.partial(kernel, slots),
        out_shape=jax.ShapeDtypeStruct((own_pairs, orbitals, orbitals), jnp.float32),
        in_specs=[vmem, smem, vmem, vmem, vmem, pl.BlockSpec(memory_space=pl.ANY), vmem, smem, vmem],
        out_specs=pl.BlockSpec(memory_space=pl.ANY),
        scratch_shapes=[
            pltpu.VMEM((GROUP, own_pairs, domain, orbitals), jnp.bfloat16),
            row, row, row, row,
            amps, amps, amps,
            pltpu.VMEM(ladder_factor.shape, jnp.bfloat16),
            pltpu.VMEM((QUAD, slots) + square, jnp.bfloat16),
            pltpu.VMEM((QUAD, slots + 1) + square, jnp.float32),
            pltpu.VMEM((own_pairs,) + square, jnp.float32),
            pltpu.VMEM((ITERS, 2, own_pairs) + square, jnp.bfloat16),
            pltpu.VMEM((ITERS, own_pairs) + square, jnp.bfloat16),
            pltpu.VMEM((ITERS, 2, own_pairs) + square, jnp.bfloat16),
            pltpu.VMEM((ITERS, own_pairs) + square, jnp.bfloat16),
            ints, ints, floats, floats,
            pltpu.SMEM((QUAD, slots + own_pairs, 128), jnp.int32),
            dma((own_pairs,)),
            dma((ITERS + 1, 3, pieces)),
            dma((ITERS + 1,)),
            dma((ITERS + 1,)),
            dma((QUAD, pieces)),
            dma,
            dma((2, QUAD)),
            dma((2, QUAD)),
            dma((QUAD,)),
            dma((ITERS, 2, pieces)),
            dma((ITERS, pieces)),
            dma,
            dma,
            pltpu.VMEM((own_pairs,) + square, jnp.float32),
            dma,
        ],
        compiler_params=pltpu.CompilerParams(
            collective_id=0, has_side_effects=True, vmem_limit_bytes=VMEM_BYTES
        ),
        name="jacobi",
    )(
        pno_basis, pno_count, partner_owner, partner_local, exchange_k, ladder_factor,
        pno_energy, occ_energy, coupling_fock,
    )


def shards(*args):
    n = lax.axis_size("pairs")
    own_pairs, domain, orbitals = args[0].shape
    fitted, partners = args[5].shape[1], args[2].shape[1]
    square = orbitals * orbitals
    each = -(-own_pairs * partners // n)
    slots = QUAD * GROUP * each
    held = 2 * own_pairs * orbitals * domain * (GROUP + QUAD + 2) + 2 * args[5].size
    held += square * (2 * ITERS * own_pairs * (GROUP + 6) + slots * 6 + own_pairs * 24)
    fits = held < VMEM_BYTES - (4 << 20)
    exact = n == QUAD * GROUP and own_pairs * partners == n * each
    if exact and own_pairs % 8 == 0 and fitted % 2 == 0 and fits:
        return fused(n, *args)
    return gathered_rows(*args)


def gathered_rows(
    pno_basis,
    pno_count,
    partner_owner,
    partner_local,
    exchange_k,
    ladder_factor,
    pno_energy,
    occ_energy,
    coupling_fock,
):
    own_pairs, domain, orbitals = pno_basis.shape
    fitted = ladder_factor.shape[1]
    partners = partner_owner.shape[1]
    listed = own_pairs * partners
    columns = lax.broadcasted_iota(jnp.int32, (own_pairs, orbitals), 1)
    live_cols = (columns < pno_count[:, None]).astype(jnp.float32)
    masked_basis = pno_basis * live_cols[:, None, :].astype(jnp.bfloat16)
    partner = (partner_owner * own_pairs + partner_local).reshape(listed)

    def rows_of(every):
        return lax.map(lambda i: lax.dynamic_index_in_dim(every, i, 0, keepdims=False), partner)

    every_basis = lax.all_gather(masked_basis, "pairs", axis=0, tiled=True)
    partner_basis = rows_of(every_basis).reshape(own_pairs, partners, domain, orbitals)
    margin = jnp.einsum(
        "rva,rcvb->rcab", masked_basis, partner_basis, preferred_element_type=jnp.float32
    ).astype(jnp.bfloat16)
    energy_sum = pno_energy[:, :, None] + pno_energy[:, None, :] - occ_energy[:, None, None]
    divisor = energy_sum + level_shift
    driving = exchange_k.astype(jnp.float32) * (live_cols[:, :, None] * live_cols[:, None, :])
    amplitudes = -driving / divisor
    weights = coupling_fock.astype(jnp.float32)
    group_width = 8
    for iteration in range(ITERS):
        sent_amps = amplitudes.astype(jnp.bfloat16)
        every_amps = lax.all_gather(sent_amps, "pairs", axis=0, tiled=True)

        def add_group(group_index, total):
            factors = lax.dynamic_slice_in_dim(
                ladder_factor, group_index * group_width, group_width, 1
            )
            ladder_half = jnp.einsum(
                "rqac,rcd->rqad", factors, sent_amps, preferred_element_type=jnp.float32
            ).astype(jnp.bfloat16)
            return total + jnp.einsum(
                "rqad,rqbd->rab", ladder_half, factors, preferred_element_type=jnp.float32
            )

        ladder = lax.fori_loop(
            0,
            fitted // group_width,
            add_group,
            jnp.zeros((own_pairs, orbitals, orbitals), jnp.float32),
        )
        partner_amps = rows_of(every_amps)
        partner_amps = partner_amps.reshape(own_pairs, partners, orbitals, orbitals)
        left_half = jnp.einsum(
            "rcab,rcbd->rcad", margin, partner_amps, preferred_element_type=jnp.float32
        )
        left_half = (left_half * weights[:, :, None, None]).astype(jnp.bfloat16)
        gathered_terms = jnp.einsum(
            "rcad,rced->rcae", left_half, margin, preferred_element_type=jnp.float32
        ).astype(jnp.bfloat16)
        coupled = jnp.sum(gathered_terms, axis=1, dtype=jnp.float32)
        residual = driving + energy_sum * amplitudes + coupled + ladder
        amplitudes = amplitudes - residual / divisor
    return amplitudes


def solution(mesh):
    return jax.shard_map(
        shards,
        mesh=mesh,
        in_specs=(
            P("pairs", None, None),
            P("pairs"),
            P("pairs", None),
            P("pairs", None),
            P("pairs", None, None),
            P("pairs", None, None, None),
            P("pairs", None),
            P("pairs"),
            P("pairs", None),
        ),
        out_specs=P("pairs", None, None),
        check_vma=False,
    )
```
